32 devices in a mesh: depth: 8 (over y, x, core), plane: 4 (over z).
Axes of the slice: x: 2, y: 2, z: 4, core: 2. Of those that a mesh axis runs over, the one named last changes fastest.
Arguments:
- spectrum: bfloat16 [2, 1024, 16, 1024], P(None, 'depth', 'plane'), may hold values from -6 to 6
- transfer_coeffs: float32 [8, 4, 4], replicated, may hold values from -3 to 3
- transfer_index: int32 [8], replicated, may hold values from 0 to 7, each once
Outputs:
- scalar_field: float32 [1024, 16, 1024], P('depth', 'plane')
- rendered: float32 [8, 4, 16, 1024], P(None, None, 'plane', 'depth')
The draws below stay inside these ranges and needn't reach their ends.
Inputs may be any that keep to these rules, and one draw needn't show every extreme that they name: `transfer_index`: each transfer function is used by exactly one image.
All inputs are finite; a program needn't handle non-finite values.
Results may differ from the reference program's by a relative error of at most 0.0003.
Values may be sent and summed in bfloat16 or wider, within the bound.
No kernel may reach another device: no remote copies, remote signals or barrier semaphores. Data moves between devices by JAX's collectives and lax.ppermute only.
A program may use at most 64 MiB of HBM per device.

```python
import jax
import jax.numpy as jnp
from jax import lax

NX = 1024
NZ = 1024
TFS = 8
COEFS = 4
IMAGES = 8
NY = 16


def shard_levels(own_key, extent, cuts, least, high):
    def one(position, parts):
        draws = jax.random.uniform(jax.random.fold_in(jax.random.fold_in(own_key, 6), position), (parts,), jnp.float32, least / len(cuts), high / len(cuts))
        return jnp.repeat(jnp.exp(draws), extent[position] // parts).reshape((-1,) + (1,) * (len(extent) - position - 1))

    gain = one(*cuts[0])
    for cut in cuts[1:]:
        gain = gain * one(*cut)
    return gain


def bell_draw(stream_key, shape, deviation, reach, pieces=(), kind=jnp.bfloat16):
    entries = jax.random.normal(stream_key, shape, jnp.float32) * deviation
    if len(pieces) > 0:
        entries = shard_levels(stream_key, shape, pieces, -0.22, 0.18) * entries
    return jnp.clip(entries, min=-reach, max=reach).astype(kind)


def setup_inputs(seed: int = 0) -> dict:
    keys = jax.random.split(jax.random.key(seed), 4)
    return {
        "spectrum": bell_draw(keys[0], (2, NZ, NY, NX), 1.0, 6.0, ((1, 8), (2, 4))),
        "transfer_coeffs": bell_draw(keys[1], (TFS, 4, COEFS), 0.5, 3.0, (), jnp.float32),
        "transfer_index": jax.random.permutation(keys[2], TFS).astype(jnp.int32),
    }


density = 2.0
shade_gain = 0.4
highest = lax.Precision.HIGHEST

def dft_tables(length):
    indices = jnp.arange(length, dtype=jnp.int32)
    phase_index = indices[:, None] * indices[None, :] % length
    angles = phase_index.astype(jnp.float32) * (2.0 * jnp.pi / length)
    scaling = 1.0 / jnp.sqrt(jnp.float32(length))
    return (jnp.cos(angles) * scaling, jnp.sin(angles) * scaling)

def polynomial(coeffs, values):
    result = coeffs[-1] + jnp.zeros_like(values)
    for degree in range(coeffs.shape[0] - 2, -1, -1):
        result = result * values + coeffs[degree]
    return result

def reference(spectrum, transfer_coeffs, transfer_index):
    cos_z, sin_z = dft_tables(NZ)
    cos_x, sin_x = dft_tables(NX)

    def plane_field(plane_modes):
        real_part = plane_modes[0].astype(jnp.float32)
        imag_part = plane_modes[1].astype(jnp.float32)
        g_re = jnp.dot(cos_z, real_part, precision=highest) - jnp.dot(sin_z, imag_part, precision=highest)
        g_im = jnp.dot(sin_z, real_part, precision=highest) + jnp.dot(cos_z, imag_part, precision=highest)
        return jnp.dot(g_re, cos_x, precision=highest) - jnp.dot(g_im, sin_x, precision=highest)
    per_plane = lax.map(plane_field, jnp.transpose(spectrum, (2, 0, 1, 3)))
    scalar_field = jnp.transpose(per_plane, (1, 0, 2))
    slope_cells = 0.5 * (jnp.roll(per_plane, -1, 0) - jnp.roll(per_plane, 1, 0))
    selected = transfer_coeffs[transfer_index]

    def plane_image(pair):
        values, slope_plane = pair
        lighting = 1.0 + shade_gain * jnp.tanh(slope_plane)
        per_image = []
        for which_image in range(IMAGES):
            coeffs = selected[which_image]
            optical = jax.nn.softplus(polynomial(coeffs[3], values)) * (density / NZ)
            before = jnp.cumsum(optical, axis=0) - optical
            weight = jnp.exp(-before) * -jnp.expm1(-optical) * lighting
            channels = []
            for channel in range(3):
                glow_cells = jax.nn.softplus(polynomial(coeffs[channel], values))
                channels.append(lax.optimization_barrier(jnp.sum(weight * glow_cells, axis=0)))
            channels.append(jnp.exp(-lax.optimization_barrier(jnp.sum(optical, axis=0))))
            per_image.append(jnp.stack(channels))
        return jnp.stack(per_image)
    images = lax.map(plane_image, (per_plane, slope_cells))
    return (scalar_field, jnp.transpose(images, (1, 2, 0, 3)))
```

```python
import functools

import jax
import jax.numpy as jnp
import numpy as np
from jax import lax
from jax.experimental import pallas as pl
from jax.experimental.pallas import tpu as pltpu
from jax.sharding import PartitionSpec as P

density = 2.0
shade_gain = 0.4
highest = lax.Precision.HIGHEST
LANES = 128
SEGS = 8
RADIX = 4
LOG2E = 1.4426950408889634
LN2 = 0.6931471805599453


def split_table(table):
    hi = table.astype(jnp.bfloat16)
    lo = (table - hi.astype(np.float64)).astype(jnp.bfloat16)
    return jnp.asarray(hi), jnp.asarray(lo)


def x_tables(nx, blocks):
    k = np.arange(nx, dtype=np.int64)
    angle = 2.0 * np.pi * ((k[:, None] * k[None, :]) % nx) / nx
    cols = nx // blocks
    cos = (np.cos(angle) / np.sqrt(nx)).reshape(nx, blocks, cols)
    sin = (np.sin(angle) / np.sqrt(nx)).reshape(nx, blocks, cols)
    return split_table(np.concatenate([cos, sin], axis=2).transpose(1, 0, 2))


def z_tables(nz):
    quarter = nz // RADIX
    q = np.arange(quarter, dtype=np.int64)
    steps = quarter // SEGS
    row = np.arange(quarter)
    m = (row % SEGS) * steps + row // SEGS
    angle = 2.0 * np.pi * ((m[:, None] * q[None, :]) % quarter) / quarter
    table = np.concatenate([np.cos(angle), -np.sin(angle)], axis=1) / np.sqrt(nz)
    turn = 2.0 * np.pi * np.arange(1, RADIX)[:, None] * q[None, :] / nz
    twiddle = np.stack([np.cos(turn), np.sin(turn)], axis=1)
    wide = np.broadcast_to(twiddle[..., None], twiddle.shape + (LANES,))
    return split_table(table) + (jnp.asarray(wide, jnp.float32),)


def x_kernel(spec_ref, hi_ref, lo_ref, out_ref):
    planes, _, rows, cols = out_ref.shape[1:]
    hi = hi_ref[0]
    lo = lo_ref[0]

    def product(part, plane):
        modes = spec_ref[part, plane]
        return jnp.dot(modes, hi, preferred_element_type=jnp.float32) + jnp.dot(
            modes, lo, preferred_element_type=jnp.float32
        )

    for plane in range(planes):
        a = product(0, plane)
        b = product(1, plane)
        out_ref[0, plane, 0] = a[:, :cols] - b[:, cols:]
        out_ref[0, plane, 1] = a[:, cols:] + b[:, :cols]


def x_transform(spec, hi, lo):
    parts, planes, rows, nx = spec.shape
    blocks, _, wide = hi.shape
    cols = wide // 2
    return pl.pallas_call(
        x_kernel,
        grid=(blocks,),
        in_specs=[
            pl.BlockSpec((parts, planes, rows, nx), lambda d: (0, 0, 0, 0)),
            pl.BlockSpec((1, nx, wide), lambda d: (d, 0, 0)),
            pl.BlockSpec((1, nx, wide), lambda d: (d, 0, 0)),
        ],
        out_specs=pl.BlockSpec((1, planes, 2, rows, cols), lambda d: (d, 0, 0, 0, 0)),
        out_shape=jax.ShapeDtypeStruct((blocks, planes, 2, rows, cols), jnp.float32),
        cost_estimate=pl.CostEstimate(
            flops=2 * parts * planes * rows * nx * nx * 4,
            bytes_accessed=12 * 2**20,
            transcendentals=0,
        ),
        name="x_transform",
    )(spec, hi, lo)


def z_kernel(in_ref, hi_ref, lo_ref, twiddle_ref, out_ref, yhi_ref, ylo_ref):
    blocks, _, _, rows, cols = in_ref.shape
    quarter = hi_ref.shape[0]
    per = quarter // rows

    def split(value, row, rank):
        high = value.astype(jnp.bfloat16)
        yhi_ref[pl.ds(row, rows), rank * cols : (rank + 1) * cols] = high
        ylo_ref[pl.ds(row, rows), rank * cols : (rank + 1) * cols] = (
            value - high.astype(jnp.float32)
        ).astype(jnp.bfloat16)

    for block in range(per):
        re = [in_ref[t * per + block, 0, 0] for t in range(RADIX)]
        im = [in_ref[t * per + block, 0, 1] for t in range(RADIX)]
        row = block * rows
        even_re, even_im = re[0] + re[2], im[0] + im[2]
        diff_re, diff_im = re[0] - re[2], im[0] - im[2]
        odd_re, odd_im = re[1] + re[3], im[1] + im[3]
        side_re, side_im = re[1] - re[3], im[1] - im[3]
        sums = (
            (even_re + odd_re, even_im + odd_im),
            (diff_re - side_im, diff_im + side_re),
            (even_re - odd_re, even_im - odd_im),
            (diff_re + side_im, diff_im - side_re),
        )
        for rank in range(RADIX):
            a, b = sums[rank]
            if rank > 0:
                c = twiddle_ref[rank - 1, 0, pl.ds(row, rows)]
                s = twiddle_ref[rank - 1, 1, pl.ds(row, rows)]
                a, b = a * c - b * s, a * s + b * c
            split(a, row, rank)
            split(b, quarter + row, rank)
    hi = hi_ref[...]
    lo = lo_ref[...]
    yhi = yhi_ref[...]
    ylo = ylo_ref[...]
    total = (
        jnp.dot(hi, yhi, preferred_element_type=jnp.float32)
        + jnp.dot(hi, ylo, preferred_element_type=jnp.float32)
        + jnp.dot(lo, yhi, preferred_element_type=jnp.float32)
    )
    for rank in range(RADIX):
        out_ref[0, rank] = total[:, rank * cols : (rank + 1) * cols]


def z_transform(arrived, hi, lo, twiddle):
    blocks, planes, _, rows, cols = arrived.shape
    quarter = hi.shape[0]
    return pl.pallas_call(
        z_kernel,
        grid=(planes,),
        in_specs=[
            pl.BlockSpec((blocks, 1, 2, rows, cols), lambda p: (0, p, 0, 0, 0)),
            pl.BlockSpec(hi.shape, lambda p: (0, 0)),
            pl.BlockSpec(lo.shape, lambda p: (0, 0)),
            pl.BlockSpec(twiddle.shape, lambda p: (0, 0, 0, 0)),
        ],
        out_specs=pl.BlockSpec((1, RADIX, quarter, cols), lambda p: (p, 0, 0, 0)),
        out_shape=jax.ShapeDtypeStruct((planes, RADIX, quarter, cols), jnp.float32),
        scratch_shapes=[
            pltpu.VMEM((2 * quarter, RADIX * cols), jnp.bfloat16),
            pltpu.VMEM((2 * quarter, RADIX * cols), jnp.bfloat16),
        ],
        cost_estimate=pl.CostEstimate(
            flops=2 * planes * quarter * 2 * quarter * RADIX * cols * 3,
            bytes_accessed=6 * 2**20,
            transcendentals=0,
        ),
        name="z_transform",
    )(arrived, hi, lo, twiddle)


def soft2(coeffs, value):
    power = ((coeffs[3] * value + coeffs[2]) * value + coeffs[1]) * value + coeffs[0]
    grown = jnp.exp2(jnp.minimum(power, 126.0))
    large = jnp.log2(1.0 + grown)
    soft = jnp.where(grown < 2.0**-12, grown * LOG2E, large)
    return jnp.maximum(soft, power)


def render_kernel(cells, coeffs_ref, index_ref, *refs):
    planes = len(refs) - 4
    field_refs = refs[:planes]
    before_ref, after_ref, out_ref, light_ref = refs[planes:]
    steps = field_refs[0].shape[1] // SEGS
    images = index_ref.shape[0]
    chain = [before_ref, *field_refs, after_ref]
    shape = (SEGS, LANES)
    for plane in range(planes):
        below, here, above = chain[plane], chain[plane + 1], chain[plane + 2]

        def light(i, carry):
            rows = pl.ds(pl.multiple_of(i * SEGS, SEGS), SEGS)
            for rank in range(RADIX):
                slope = 0.5 * (above[rank, rows] - below[rank, rows])
                light_ref[rank, rows] = 1.0 + shade_gain * jnp.tanh(slope)
            return carry

        lax.fori_loop(0, steps, light, 0, unroll=2)

        def image(m, carry):
            which = index_ref[m]
            table = [
                [jnp.full(shape, coeffs_ref[which, j, n] * LOG2E, jnp.float32) for n in range(4)]
                for j in range(4)
            ]

            def step(i, state):
                clear, sums = state
                rows = pl.ds(pl.multiple_of(i * SEGS, SEGS), SEGS)
                for rank in range(RADIX):
                    value = here[rank, rows]
                    depth = soft2(table[3], value) * (density / cells * LN2)
                    passed = jnp.exp2(depth * -LOG2E)
                    taken = jnp.where(depth < 2.0**-9, depth * (1.0 - 0.5 * depth), 1.0 - passed)
                    weight = clear * taken * light_ref[rank, rows]
                    clear = clear * passed
                    sums = [acc + weight * soft2(table[j], value) for j, acc in enumerate(sums)]
                return clear, sums

            zero = jnp.zeros(shape, jnp.float32)
            clear, sums = lax.fori_loop(
                0, steps, step, (jnp.ones(shape, jnp.float32), [zero, zero, zero]), unroll=2
            )
            reach = clear[0:1]
            totals = [acc[0:1] for acc in sums]
            for seg in range(1, SEGS):
                totals = [t + reach * acc[seg : seg + 1] for t, acc in zip(totals, sums)]
                reach = reach * clear[seg : seg + 1]
            for j in range(3):
                out_ref[m, j, plane : plane + 1] = totals[j] * LN2
            out_ref[m, 3, plane : plane + 1] = reach
            return carry

        lax.fori_loop(0, images, image, 0)


def render(cells, fields, before, after, coeffs, index):
    planes = len(fields)
    images = index.shape[0]
    vmem = pl.BlockSpec(memory_space=pltpu.VMEM)
    smem = pl.BlockSpec(memory_space=pltpu.SMEM)
    return pl.pallas_call(
        functools.partial(render_kernel, cells),
        in_specs=[smem, smem] + [vmem] * (planes + 2),
        out_specs=vmem,
        out_shape=jax.ShapeDtypeStruct((images, 4, planes, LANES), jnp.float32),
        scratch_shapes=[pltpu.VMEM(fields[0].shape, jnp.float32)],
        cost_estimate=pl.CostEstimate(
            flops=64 * images * planes * cells * LANES,
            bytes_accessed=4 * (planes + 2) * cells * LANES,
            transcendentals=9 * images * planes * cells * LANES,
        ),
        name="render",
    )(coeffs, index, *fields, before, after)


def shifts(axis):
    devices = lax.axis_size(axis)
    up = [(i, (i + 1) % devices) for i in range(devices)]
    return up, [(j, i) for i, j in up]


def fast_body(spectrum, transfer_coeffs, transfer_index):
    _, rows, planes, nx = spectrum.shape
    blocks = lax.axis_size("depth")
    nz = rows * blocks
    xhi, xlo = x_tables(nx, blocks)
    zhi, zlo, twiddle = z_tables(nz)
    groups = [[0, planes - 1], list(range(1, planes - 1))]
    fields = [None] * planes
    sent = []
    for group in groups:
        picked = jnp.stack([spectrum[:, :, p] for p in group], axis=1)
        mixed = x_transform(picked, xhi, xlo)
        sent.append(lax.all_to_all(mixed, "depth", split_axis=0, concat_axis=0, tiled=True))
    halos = None
    up, down = shifts("plane")
    for group, arrived in zip(groups, sent):
        done = z_transform(arrived, zhi, zlo, twiddle)
        for at, p in enumerate(group):
            fields[p] = done[at]
        if halos is None:
            halos = (lax.ppermute(fields[-1], "plane", up), lax.ppermute(fields[0], "plane", down))
    steps = nz // RADIX // SEGS
    stacked = jnp.stack(fields).reshape(planes, RADIX, steps, SEGS, LANES)
    slabs = stacked.transpose(3, 2, 1, 0, 4).reshape(nz, planes, LANES)
    scalar_field = lax.all_to_all(slabs, "depth", split_axis=0, concat_axis=2, tiled=True)
    rendered = render(nz, fields, *halos, transfer_coeffs, transfer_index)
    return scalar_field, rendered


def with_halo(array, sides, width):
    for axis, dim in sides:
        devices, length = (lax.axis_size(axis), array.shape[dim])
        up = [(i, (i + 1) % devices) for i in range(devices)]
        down = [(j, i) for i, j in up]
        last = lax.slice_in_dim(array, length - width, length, axis=dim)
        first = lax.slice_in_dim(array, 0, width, axis=dim)
        before = lax.ppermute(last, axis, up)
        after = lax.ppermute(first, axis, down)
        array = jnp.concatenate([before, array, after], axis=dim)
    return array


def dft_tables(length):
    indices = jnp.arange(length, dtype=jnp.int32)
    phase_index = indices[:, None] * indices[None, :] % length
    angles = phase_index.astype(jnp.float32) * (2.0 * jnp.pi / length)
    scaling = 1.0 / jnp.sqrt(jnp.float32(length))
    return (jnp.cos(angles) * scaling, jnp.sin(angles) * scaling)


def polynomial(coeffs, values):
    result = coeffs[-1] + jnp.zeros_like(values)
    for degree in range(coeffs.shape[0] - 2, -1, -1):
        result = result * values + coeffs[degree]
    return result


def plane_slope(field_cells):
    padded = with_halo(field_cells, (("plane", 1),), 1)
    return 0.5 * (padded[:, 2:] - padded[:, :-2])


def render_blocks(field_cells, slope_cells, selected, blocks):
    depth_cells, plane_count, column_count = field_cells.shape
    block_cells = depth_cells // blocks
    values = field_cells.reshape(blocks, block_cells, plane_count, column_count)
    lighting = 1.0 + shade_gain * jnp.tanh(
        slope_cells.reshape(blocks, block_cells, plane_count, column_count)
    )
    per_image = []
    for which_image in range(selected.shape[0]):
        coeffs = selected[which_image]
        optical = jax.nn.softplus(polynomial(coeffs[3], values)) * (density / depth_cells)
        before = jnp.cumsum(optical, axis=1) - optical
        weight = jnp.exp(-before) * -jnp.expm1(-optical) * lighting
        block_depth = jnp.sum(optical, axis=1)
        ahead = jnp.cumsum(block_depth, axis=0) - block_depth
        reach = jnp.exp(-ahead)
        channels = []
        for channel in range(3):
            glow_cells = jax.nn.softplus(polynomial(coeffs[channel], values))
            channels.append(jnp.sum(reach * jnp.sum(weight * glow_cells, axis=1), axis=0))
        channels.append(jnp.sum(block_depth, axis=0))
        per_image.append(jnp.stack(channels))
    return jnp.stack(per_image)


def body(spectrum, transfer_coeffs, transfer_index):
    _, rows, _, nx = spectrum.shape
    cos_z, sin_z = dft_tables(rows * lax.axis_size("depth"))
    cos_x, sin_x = dft_tables(nx)
    one_hot = (
        transfer_index[:, None] == jnp.arange(transfer_coeffs.shape[0], dtype=jnp.int32)[None, :]
    ).astype(jnp.float32)
    selected = jnp.sum(one_hot[:, :, None, None] * transfer_coeffs[None], axis=1)
    depth_count = lax.axis_size("depth")
    real_part = spectrum[0].astype(jnp.float32)
    imag_part = spectrum[1].astype(jnp.float32)
    h_re = jnp.einsum("zpk,kx->zpx", real_part, cos_x, precision=highest) - jnp.einsum(
        "zpk,kx->zpx", imag_part, sin_x, precision=highest
    )
    h_im = jnp.einsum("zpk,kx->zpx", real_part, sin_x, precision=highest) + jnp.einsum(
        "zpk,kx->zpx", imag_part, cos_x, precision=highest
    )
    mixed = jnp.stack([h_re, h_im])
    arrived = lax.all_to_all(mixed, "depth", split_axis=3, concat_axis=1, tiled=True)
    field_columns = jnp.einsum("zk,kpx->zpx", cos_z, arrived[0], precision=highest) - jnp.einsum(
        "zk,kpx->zpx", sin_z, arrived[1], precision=highest
    )
    slope_cells = plane_slope(field_columns)
    merged = render_blocks(field_columns, slope_cells, selected, depth_count)
    scalar_field = lax.all_to_all(field_columns, "depth", split_axis=0, concat_axis=2, tiled=True)
    rendered = jnp.concatenate([merged[:, :3], jnp.exp(-merged[:, 3:4])], axis=1)
    return (scalar_field, rendered)


def solution(mesh):
    def pick(spectrum, *rest):
        _, rows, planes, nx = spectrum.shape
        blocks = lax.axis_size("depth")
        if nx == LANES * blocks and blocks % RADIX == 0 and planes > 3 and rows % 16 == 0:
            return fast_body(spectrum, *rest)
        return body(spectrum, *rest)

    return jax.shard_map(
        pick,
        mesh=mesh,
        in_specs=(P(None, "depth", "plane", None), P(), P()),
        out_specs=(P("depth", "plane", None), P(None, None, "plane", "depth")),
        check_vma=False,
    )
```

```python
import functools

import jax
import jax.numpy as jnp
import numpy as np
from jax import lax
from jax.experimental import pallas as pl
from jax.experimental.pallas import tpu as pltpu
from jax.sharding import PartitionSpec as P

density = 2.0
shade_gain = 0.4
highest = lax.Precision.HIGHEST
LANES = 128
SEGS = 8
RADIX = 4
PACK = 16
LEVELS = 16.0
STEPS = 32766.0
TINY = 2.0**-108
LOG2E = 1.4426950408889634
LN2 = 0.6931471805599453


def split_table(table):
    hi = table.astype(jnp.bfloat16)
    lo = (table - hi.astype(np.float64)).astype(jnp.bfloat16)
    return jnp.asarray(hi), jnp.asarray(lo)


def x_tables(nx, blocks):
    k = np.arange(nx, dtype=np.int64)
    angle = 2.0 * np.pi * ((k[:, None] * k[None, :]) % nx) / nx
    cols = nx // blocks
    cos = (np.cos(angle) / np.sqrt(nx)).reshape(nx, blocks, cols)
    sin = (np.sin(angle) / np.sqrt(nx)).reshape(nx, blocks, cols)
    return split_table(np.concatenate([cos, sin], axis=2).transpose(1, 0, 2))


def z_tables(nz):
    quarter = nz // RADIX
    q = np.arange(quarter, dtype=np.int64)
    steps = quarter // SEGS
    row = np.arange(quarter)
    m = (row % SEGS) * steps + row // SEGS
    angle = 2.0 * np.pi * ((m[:, None] * q[None, :]) % quarter) / quarter
    table = np.concatenate([np.cos(angle), -np.sin(angle)], axis=1) / np.sqrt(nz)
    turn = 2.0 * np.pi * np.arange(1, RADIX)[:, None] * q[None, :] / nz
    twiddle = np.stack([np.cos(turn), np.sin(turn)], axis=1)
    wide = np.broadcast_to(twiddle[..., None], twiddle.shape + (LANES,))
    return split_table(table) + (jnp.asarray(wide, jnp.float32),)


def x_kernel(planes, spec_ref, hi_ref, lo_ref, out_ref, mixed_ref):
    half = spec_ref.shape[0] // 2
    rows = half // planes
    cols = hi_ref.shape[2] // 2
    hi = hi_ref[0]
    lo = lo_ref[0]

    def product(part):
        modes = spec_ref[part * half : (part + 1) * half]
        return jnp.dot(modes, hi, preferred_element_type=jnp.float32) + jnp.dot(
            modes, lo, preferred_element_type=jnp.float32
        )

    a = product(0)
    b = product(1)
    mixed_ref[0] = a[:, :cols] - b[:, cols:]
    mixed_ref[1] = a[:, cols:] + b[:, :cols]
    levels = jnp.zeros((PACK, cols), jnp.float32)
    place = lax.broadcasted_iota(jnp.int32, (PACK, cols), 0)
    for plane in range(planes):
        parts = [mixed_ref[part, pl.ds(plane, rows, stride=planes)] for part in range(2)]
        peak = jnp.maximum(jnp.abs(parts[0]), jnp.abs(parts[1]))
        peak = jnp.max(peak, axis=0, keepdims=True)
        level = jnp.ceil(LEVELS * jnp.log2(jnp.maximum(peak, TINY))) + 1.0
        scale = STEPS * jnp.exp2(level * (-1.0 / LEVELS))
        for part in range(2):
            at = (plane * 2 + part) * rows
            whole = jnp.round(parts[part] * scale).astype(jnp.int32)
            out_ref[0, at : at + rows] = whole.astype(jnp.int16)
        levels = jnp.where(place == plane, jnp.broadcast_to(level, levels.shape), levels)
    at = planes * 2 * rows
    out_ref[0, at : at + PACK] = levels.astype(jnp.int32).astype(jnp.int16)


def x_transform(spec, planes, hi, lo):
    modes, nx = spec.shape
    blocks, _, wide = hi.shape
    cols = wide // 2
    return pl.pallas_call(
        functools.partial(x_kernel, planes),
        grid=(blocks,),
        in_specs=[
            pl.BlockSpec((modes, nx), lambda d: (0, 0)),
            pl.BlockSpec((1, nx, wide), lambda d: (d, 0, 0)),
            pl.BlockSpec((1, nx, wide), lambda d: (d, 0, 0)),
        ],
        out_specs=pl.BlockSpec((1, modes + PACK, cols), lambda d: (d, 0, 0)),
        out_shape=jax.ShapeDtypeStruct((blocks, modes + PACK, cols), jnp.int16),
        scratch_shapes=[pltpu.VMEM((2, modes // 2, cols), jnp.float32)],
        cost_estimate=pl.CostEstimate(
            flops=2 * modes * nx * nx * 4, bytes_accessed=12 * 2**20, transcendentals=0
        ),
        name="x_transform",
    )(spec, hi, lo)


def z_kernel(
    in_ref, level_ref, hi_ref, lo_ref, twiddle_ref, out_ref, low_ref, high_ref, slab_ref,
    yhi_ref, ylo_ref,
):
    plane = pl.program_id(0)
    planes = pl.num_programs(0)
    blocks, double, cols = in_ref.shape
    rows = double // 2
    quarter = hi_ref.shape[0]
    per = quarter // rows

    def split(value, row, rank):
        high = value.astype(jnp.bfloat16)
        yhi_ref[pl.ds(row, rows), rank * cols : (rank + 1) * cols] = high
        ylo_ref[pl.ds(row, rows), rank * cols : (rank + 1) * cols] = (
            value - high.astype(jnp.float32)
        ).astype(jnp.bfloat16)

    place = lax.broadcasted_iota(jnp.int32, (PACK, cols), 0)

    def load(source, part):
        level = level_ref[source].astype(jnp.int32).astype(jnp.float32)
        level = jnp.sum(jnp.where(place == plane, level, 0.0), axis=0, keepdims=True)
        scale = jnp.exp2(level * (1.0 / LEVELS)) * (1.0 / STEPS)
        whole = in_ref[source, part * rows : (part + 1) * rows]
        return whole.astype(jnp.int32).astype(jnp.float32) * scale

    for block in range(per):
        re = [load(t * per + block, 0) for t in range(RADIX)]
        im = [load(t * per + block, 1) for t in range(RADIX)]
        row = block * rows
        even_re, even_im = re[0] + re[2], im[0] + im[2]
        diff_re, diff_im = re[0] - re[2], im[0] - im[2]
        odd_re, odd_im = re[1] + re[3], im[1] + im[3]
        side_re, side_im = re[1] - re[3], im[1] - im[3]
        sums = (
            (even_re + odd_re, even_im + odd_im),
            (diff_re - side_im, diff_im + side_re),
            (even_re - odd_re, even_im - odd_im),
            (diff_re + side_im, diff_im - side_re),
        )
        for rank in range(RADIX):
            a, b = sums[rank]
            if rank > 0:
                c = twiddle_ref[rank - 1, 0, pl.ds(row, rows)]
                s = twiddle_ref[rank - 1, 1, pl.ds(row, rows)]
                a, b = a * c - b * s, a * s + b * c
            split(a, row, rank)
            split(b, quarter + row, rank)
    hi = hi_ref[...]
    lo = lo_ref[...]
    yhi = yhi_ref[...]
    ylo = ylo_ref[...]
    total = (
        jnp.dot(hi, yhi, preferred_element_type=jnp.float32)
        + jnp.dot(hi, ylo, preferred_element_type=jnp.float32)
        + jnp.dot(lo, yhi, preferred_element_type=jnp.float32)
    )
    for rank in range(RADIX):
        out_ref[0, rank] = total[:, rank * cols : (rank + 1) * cols]

    @pl.when(plane == 0)
    def _():
        low_ref[...] = out_ref[0]

    @pl.when(plane == planes - 1)
    def _():
        high_ref[...] = out_ref[0]

    steps = quarter // SEGS
    count = slab_ref.shape[1] // (RADIX * steps)
    for seg in range(SEGS):
        for rank in range(RADIX):
            values = out_ref[0, rank, pl.ds(seg, steps, stride=SEGS)]
            slab_ref[seg, pl.ds(rank * count + plane, steps, stride=RADIX * count)] = values


def z_transform(arrived, planes, hi, lo, twiddle):
    blocks, total, cols = arrived.shape
    double = (total - PACK) // planes
    quarter = hi.shape[0]
    field = (RADIX, quarter, cols)
    last = planes * double // PACK
    return pl.pallas_call(
        z_kernel,
        grid=(planes,),
        in_specs=[
            pl.BlockSpec((blocks, double, cols), lambda p: (0, p, 0)),
            pl.BlockSpec((blocks, PACK, cols), lambda p: (0, last, 0)),
            pl.BlockSpec(hi.shape, lambda p: (0, 0)),
            pl.BlockSpec(lo.shape, lambda p: (0, 0)),
            pl.BlockSpec(twiddle.shape, lambda p: (0, 0, 0, 0)),
        ],
        out_specs=[
            pl.BlockSpec((1, *field), lambda p: (p, 0, 0, 0)),
            pl.BlockSpec(field, lambda p: (0, 0, 0)),
            pl.BlockSpec(field, lambda p: (0, 0, 0)),
            pl.BlockSpec((SEGS, RADIX * quarter // SEGS * planes, cols), lambda p: (0, 0, 0)),
        ],
        out_shape=[
            jax.ShapeDtypeStruct((planes, *field), jnp.float32),
            jax.ShapeDtypeStruct(field, jnp.float32),
            jax.ShapeDtypeStruct(field, jnp.float32),
            jax.ShapeDtypeStruct((SEGS, RADIX * quarter // SEGS * planes, cols), jnp.float32),
        ],
        scratch_shapes=[
            pltpu.VMEM((2 * quarter, RADIX * cols), jnp.bfloat16),
            pltpu.VMEM((2 * quarter, RADIX * cols), jnp.bfloat16),
        ],
        cost_estimate=pl.CostEstimate(
            flops=2 * planes * quarter * 2 * quarter * RADIX * cols * 3,
            bytes_accessed=6 * 2**20,
            transcendentals=0,
        ),
        name="z_transform",
    )(arrived, arrived, hi, lo, twiddle)


def soft2(coeffs, value):
    power = ((coeffs[3] * value + coeffs[2]) * value + coeffs[1]) * value + coeffs[0]
    grown = jnp.exp2(jnp.minimum(power, 126.0))
    large = jnp.log2(1.0 + grown)
    soft = jnp.where(grown < 2.0**-12, grown * LOG2E, large)
    return jnp.maximum(soft, power)


def render_kernel(cells, picked, coeffs_ref, index_ref, field_ref, *refs):
    edges, (out_ref, light_ref) = refs[:-2], refs[-2:]
    steps = field_ref.shape[2] // SEGS
    images = index_ref.shape[0]
    last = field_ref.shape[0] - 1
    shape = (SEGS, LANES)
    if edges:
        done_ref, before_ref, after_ref = edges
        out_ref[...] = done_ref[...]
    for plane in picked:
        here = field_ref.at[plane]
        below = before_ref if plane == 0 else field_ref.at[plane - 1]
        above = after_ref if plane == last else field_ref.at[plane + 1]

        def light(i, carry):
            rows = pl.ds(pl.multiple_of(i * SEGS, SEGS), SEGS)
            for rank in range(RADIX):
                slope = 0.5 * (above[rank, rows] - below[rank, rows])
                light_ref[rank, rows] = 1.0 + shade_gain * jnp.tanh(slope)
            return carry

        lax.fori_loop(0, steps, light, 0, unroll=2)

        def image(m, carry):
            which = index_ref[m]
            table = [
                [jnp.full(shape, coeffs_ref[which, j, n] * LOG2E, jnp.float32) for n in range(4)]
                for j in range(4)
            ]

            def step(i, state):
                clear, sums = state
                rows = pl.ds(pl.multiple_of(i * SEGS, SEGS), SEGS)
                for rank in range(RADIX):
                    value = here[rank, rows]
                    depth = soft2(table[3], value) * (density / cells * LN2)
                    passed = jnp.exp2(depth * -LOG2E)
                    taken = jnp.where(depth < 2.0**-9, depth * (1.0 - 0.5 * depth), 1.0 - passed)
                    weight = clear * taken * light_ref[rank, rows]
                    clear = clear * passed
                    sums = [acc + weight * soft2(table[j], value) for j, acc in enumerate(sums)]
                return clear, sums

            zero = jnp.zeros(shape, jnp.float32)
            clear, sums = lax.fori_loop(
                0, steps, step, (jnp.ones(shape, jnp.float32), [zero, zero, zero]), unroll=2
            )
            reach = clear[0:1]
            totals = [acc[0:1] for acc in sums]
            for seg in range(1, SEGS):
                totals = [t + reach * acc[seg : seg + 1] for t, acc in zip(totals, sums)]
                reach = reach * clear[seg : seg + 1]
            for j in range(3):
                out_ref[m, j, plane : plane + 1] = totals[j] * LN2
            out_ref[m, 3, plane : plane + 1] = reach
            return carry

        lax.fori_loop(0, images, image, 0)


def render(cells, picked, coeffs, index, fields, *edges):
    images = index.shape[0]
    planes = fields.shape[0]
    vmem = pl.BlockSpec(memory_space=pltpu.VMEM)
    smem = pl.BlockSpec(memory_space=pltpu.SMEM)
    points = images * len(picked) * cells * LANES
    return pl.pallas_call(
        functools.partial(render_kernel, cells, picked),
        in_specs=[smem, smem, vmem] + [vmem] * len(edges),
        out_specs=vmem,
        out_shape=jax.ShapeDtypeStruct((images, 4, planes, LANES), jnp.float32),
        scratch_shapes=[pltpu.VMEM(fields.shape[1:], jnp.float32)],
        cost_estimate=pl.CostEstimate(
            flops=64 * points, bytes_accessed=4 * 2**20, transcendentals=9 * points
        ),
        name="render",
    )(coeffs, index, fields, *edges)


def shifts(axis):
    devices = lax.axis_size(axis)
    up = [(i, (i + 1) % devices) for i in range(devices)]
    return up, [(j, i) for i, j in up]


def fast_body(spectrum, transfer_coeffs, transfer_index):
    _, rows, planes, nx = spectrum.shape
    blocks = lax.axis_size("depth")
    nz = rows * blocks
    xhi, xlo = x_tables(nx, blocks)
    zhi, zlo, twiddle = z_tables(nz)
    mixed = x_transform(spectrum.reshape(2 * rows * planes, nx), planes, xhi, xlo)
    arrived = lax.all_to_all(mixed, "depth", split_axis=0, concat_axis=0, tiled=True)
    fields, low, high, slabs = z_transform(arrived, planes, zhi, zlo, twiddle)
    up, down = shifts("plane")
    before = lax.ppermute(high, "plane", up)
    after = lax.ppermute(low, "plane", down)
    slabs = lax.all_to_all(
        slabs.reshape(blocks, rows, planes, LANES), "depth", split_axis=0, concat_axis=0, tiled=True
    )
    scalar_field = slabs.transpose(1, 2, 0, 3).reshape(rows, planes, nx)
    inner = tuple(range(1, planes - 1))
    picture = render(nz, inner, transfer_coeffs, transfer_index, fields)
    rendered = render(
        nz, (0, planes - 1), transfer_coeffs, transfer_index, fields, picture, before, after
    )
    return scalar_field, rendered


def with_halo(array, sides, width):
    for axis, dim in sides:
        devices, length = (lax.axis_size(axis), array.shape[dim])
        up = [(i, (i + 1) % devices) for i in range(devices)]
        down = [(j, i) for i, j in up]
        last = lax.slice_in_dim(array, length - width, length, axis=dim)
        first = lax.slice_in_dim(array, 0, width, axis=dim)
        before = lax.ppermute(last, axis, up)
        after = lax.ppermute(first, axis, down)
        array = jnp.concatenate([before, array, after], axis=dim)
    return array


def dft_tables(length):
    indices = jnp.arange(length, dtype=jnp.int32)
    phase_index = indices[:, None] * indices[None, :] % length
    angles = phase_index.astype(jnp.float32) * (2.0 * jnp.pi / length)
    scaling = 1.0 / jnp.sqrt(jnp.float32(length))
    return (jnp.cos(angles) * scaling, jnp.sin(angles) * scaling)


def polynomial(coeffs, values):
    result = coeffs[-1] + jnp.zeros_like(values)
    for degree in range(coeffs.shape[0] - 2, -1, -1):
        result = result * values + coeffs[degree]
    return result


def plane_slope(field_cells):
    padded = with_halo(field_cells, (("plane", 1),), 1)
    return 0.5 * (padded[:, 2:] - padded[:, :-2])


def render_blocks(field_cells, slope_cells, selected, blocks):
    depth_cells, plane_count, column_count = field_cells.shape
    block_cells = depth_cells // blocks
    values = field_cells.reshape(blocks, block_cells, plane_count, column_count)
    lighting = 1.0 + shade_gain * jnp.tanh(
        slope_cells.reshape(blocks, block_cells, plane_count, column_count)
    )
    per_image = []
    for which_image in range(selected.shape[0]):
        coeffs = selected[which_image]
        optical = jax.nn.softplus(polynomial(coeffs[3], values)) * (density / depth_cells)
        before = jnp.cumsum(optical, axis=1) - optical
        weight = jnp.exp(-before) * -jnp.expm1(-optical) * lighting
        block_depth = jnp.sum(optical, axis=1)
        ahead = jnp.cumsum(block_depth, axis=0) - block_depth
        reach = jnp.exp(-ahead)
        channels = []
        for channel in range(3):
            glow_cells = jax.nn.softplus(polynomial(coeffs[channel], values))
            channels.append(jnp.sum(reach * jnp.sum(weight * glow_cells, axis=1), axis=0))
        channels.append(jnp.sum(block_depth, axis=0))
        per_image.append(jnp.stack(channels))
    return jnp.stack(per_image)


def body(spectrum, transfer_coeffs, transfer_index):
    _, rows, _, nx = spectrum.shape
    cos_z, sin_z = dft_tables(rows * lax.axis_size("depth"))
    cos_x, sin_x = dft_tables(nx)
    one_hot = (
        transfer_index[:, None] == jnp.arange(transfer_coeffs.shape[0], dtype=jnp.int32)[None, :]
    ).astype(jnp.float32)
    selected = jnp.sum(one_hot[:, :, None, None] * transfer_coeffs[None], axis=1)
    depth_count = lax.axis_size("depth")
    real_part = spectrum[0].astype(jnp.float32)
    imag_part = spectrum[1].astype(jnp.float32)
    h_re = jnp.einsum("zpk,kx->zpx", real_part, cos_x, precision=highest) - jnp.einsum(
        "zpk,kx->zpx", imag_part, sin_x, precision=highest
    )
    h_im = jnp.einsum("zpk,kx->zpx", real_part, sin_x, precision=highest) + jnp.einsum(
        "zpk,kx->zpx", imag_part, cos_x, precision=highest
    )
    mixed = jnp.stack([h_re, h_im])
    arrived = lax.all_to_all(mixed, "depth", split_axis=3, concat_axis=1, tiled=True)
    field_columns = jnp.einsum("zk,kpx->zpx", cos_z, arrived[0], precision=highest) - jnp.einsum(
        "zk,kpx->zpx", sin_z, arrived[1], precision=highest
    )
    slope_cells = plane_slope(field_columns)
    merged = render_blocks(field_columns, slope_cells, selected, depth_count)
    scalar_field = lax.all_to_all(field_columns, "depth", split_axis=0, concat_axis=2, tiled=True)
    rendered = jnp.concatenate([merged[:, :3], jnp.exp(-merged[:, 3:4])], axis=1)
    return (scalar_field, rendered)


def solution(mesh):
    def pick(spectrum, *rest):
        _, rows, planes, nx = spectrum.shape
        blocks = lax.axis_size("depth")
        if nx == LANES * blocks and blocks == SEGS and planes > 2 and rows % PACK == 0:
            return fast_body(spectrum, *rest)
        return body(spectrum, *rest)

    return jax.shard_map(
        pick,
        mesh=mesh,
        in_specs=(P(None, "depth", "plane", None), P(), P()),
        out_specs=(P("depth", "plane", None), P(None, None, "plane", "depth")),
        check_vma=False,
    )
```

```python
import functools

import jax
import jax.numpy as jnp
import numpy as np
from jax import lax
from jax.experimental import pallas as pl
from jax.experimental.pallas import tpu as pltpu
from jax.sharding import PartitionSpec as P


density = 2.0
shade_gain = 0.4
highest = lax.Precision.HIGHEST
LANES = 128
SEGS = 8
RADIX = 4
PACK = 16
PAIRS = ((6, 7), (2, 4), (3, 5), (1, 0))
LEVELS = 16.0
STEPS = 32766.0
TINY = 2.0**-108
FAINT = 2.0**-9
SPARSE = 0.02
LOG2E = 1.4426950408889634
LN2 = 0.6931471805599453


def split_table(table):
    hi = table.astype(jnp.bfloat16)
    lo = (table - hi.astype(np.float64)).astype(jnp.bfloat16)
    return jnp.asarray(hi), jnp.asarray(lo)


def x_tables(nx, blocks):
    k = np.arange(nx, dtype=np.int64)
    angle = 2.0 * np.pi * ((k[:, None] * k[None, :]) % nx) / nx
    cols = nx // blocks
    cos = (np.cos(angle) / np.sqrt(nx)).reshape(nx, blocks, cols)
    sin = (np.sin(angle) / np.sqrt(nx)).reshape(nx, blocks, cols)
    return split_table(np.concatenate([cos, sin], axis=2).transpose(1, 0, 2))


def z_tables(nz):
    quarter = nz // RADIX
    q = np.arange(quarter, dtype=np.int64)
    steps = quarter // SEGS
    row = np.arange(quarter)
    m = (row % SEGS) * steps + row // SEGS
    angle = 2.0 * np.pi * ((m[:, None] * q[None, :]) % quarter) / quarter
    table = np.concatenate([np.cos(angle), -np.sin(angle)], axis=1) / np.sqrt(nz)
    turn = 2.0 * np.pi * np.arange(1, RADIX)[:, None] * q[None, :] / nz
    twiddle = np.stack([np.cos(turn), np.sin(turn)], axis=1)
    wide = np.broadcast_to(twiddle[..., None], twiddle.shape + (LANES,))
    return split_table(table) + (jnp.asarray(wide, jnp.float32),)


def x_kernel(planes, target_ref, spec_ref, hi_ref, lo_ref, *refs):
    outs, (mixed_ref,) = refs[:-1], refs[-1:]
    half = spec_ref.shape[0] // 2
    rows = half // planes
    cols = hi_ref.shape[2] // 2
    hi = hi_ref[0]
    lo = lo_ref[0]

    def product(part):
        modes = spec_ref[part * half : (part + 1) * half]
        return jnp.dot(modes, hi, preferred_element_type=jnp.float32) + jnp.dot(
            modes, lo, preferred_element_type=jnp.float32
        )

    a = product(0)
    b = product(1)
    mixed_ref[0] = a[:, :cols] - b[:, cols:]
    mixed_ref[1] = a[:, cols:] + b[:, :cols]
    place = lax.broadcasted_iota(jnp.int32, (PACK, cols), 0)

    def emit(out_ref):
        levels = jnp.zeros((PACK, cols), jnp.float32)
        for plane in range(planes):
            parts = [mixed_ref[part, pl.ds(plane, rows, stride=planes)] for part in range(2)]
            peak = jnp.maximum(jnp.abs(parts[0]), jnp.abs(parts[1]))
            peak = jnp.max(peak, axis=0, keepdims=True)
            level = jnp.ceil(LEVELS * jnp.log2(jnp.maximum(peak, TINY))) + 1.0
            scale = STEPS * jnp.exp2(level * (-1.0 / LEVELS))
            for part in range(2):
                at = (plane * 2 + part) * rows
                whole = jnp.round(parts[part] * scale).astype(jnp.int32)
                out_ref[at : at + rows] = whole.astype(jnp.int16)
            levels = jnp.where(place == plane, jnp.broadcast_to(level, levels.shape), levels)
        at = planes * 2 * rows
        out_ref[at : at + PACK] = levels.astype(jnp.int32).astype(jnp.int16)

    for which, out_ref in enumerate(outs):
        pl.when(pl.program_id(0) == which)(functools.partial(emit, out_ref))


def x_transform(spec, me, pair, planes, hi, lo):
    modes, nx = spec.shape
    _, _, wide = hi.shape
    cols = wide // 2
    count = len(pair)
    sent = (modes + PACK, cols)

    def table(d, t):
        return (jnp.bitwise_xor(t[0], jnp.where(d == 0, pair[0], pair[1])), 0, 0)

    return pl.pallas_call(
        functools.partial(x_kernel, planes),
        grid_spec=pltpu.PrefetchScalarGridSpec(
            num_scalar_prefetch=1,
            grid=(count,),
            in_specs=[
                pl.BlockSpec((modes, nx), lambda d, t: (0, 0)),
                pl.BlockSpec((1, nx, wide), table),
                pl.BlockSpec((1, nx, wide), table),
            ],
            out_specs=[pl.BlockSpec(sent, lambda d, t: (0, 0))] * count,
            scratch_shapes=[pltpu.VMEM((2, modes // 2, cols), jnp.float32)],
        ),
        out_shape=[jax.ShapeDtypeStruct(sent, jnp.int16)] * count,
        cost_estimate=pl.CostEstimate(
            flops=2 * modes * nx * wide * 2 * count,
            bytes_accessed=2 * modes * nx + 4 * nx * wide * count,
            transcendentals=0,
        ),
        name="x_transform",
    )(me, spec, hi, lo)


def z_kernel(me_ref, *refs):
    blocks = SEGS
    sent, refs = refs[:blocks], refs[blocks:]
    hi_ref, lo_ref, twiddle_ref, out_ref, low_ref, high_ref, slab_ref = refs[:7]
    in_ref, yhi_ref, ylo_ref, sem = refs[7:]
    plane = pl.program_id(0)
    planes = pl.num_programs(0)
    _, total, cols = in_ref.shape
    quarter = hi_ref.shape[0]
    rows = quarter * RADIX // blocks
    per = blocks // RADIX

    @pl.when(plane == 0)
    def _():
        copies = [
            pltpu.make_async_copy(ref, in_ref.at[jnp.bitwise_xor(me_ref[0], step)], sem.at[step])
            for step, ref in enumerate(sent)
        ]
        for copy in copies:
            copy.start()
        for copy in copies:
            copy.wait()

    def split(value, row, rank):
        high = value.astype(jnp.bfloat16)
        yhi_ref[pl.ds(row, PACK), rank * cols : (rank + 1) * cols] = high
        ylo_ref[pl.ds(row, PACK), rank * cols : (rank + 1) * cols] = (
            value - high.astype(jnp.float32)
        ).astype(jnp.bfloat16)

    place = lax.broadcasted_iota(jnp.int32, (PACK, cols), 0)

    def scale_of(source):
        level = in_ref[source, total - PACK : total].astype(jnp.int32).astype(jnp.float32)
        level = jnp.sum(jnp.where(place == plane, level, 0.0), axis=0, keepdims=True)
        return jnp.exp2(level * (1.0 / LEVELS)) * (1.0 / STEPS)

    base = pl.multiple_of(plane * (2 * rows), 2 * rows)
    for block in range(per):
        sources = [t * per + block for t in range(RADIX)]
        scales = [jnp.broadcast_to(scale_of(source), (PACK, cols)) for source in sources]

        def load(t, part, chunk):
            whole = in_ref[sources[t], pl.ds(base + part * rows + chunk, PACK)]
            return whole.astype(jnp.int32).astype(jnp.float32) * scales[t]

        for chunk in range(0, rows, PACK):
            re = [load(t, 0, chunk) for t in range(RADIX)]
            im = [load(t, 1, chunk) for t in range(RADIX)]
            row = block * rows + chunk
            even_re, even_im = re[0] + re[2], im[0] + im[2]
            diff_re, diff_im = re[0] - re[2], im[0] - im[2]
            odd_re, odd_im = re[1] + re[3], im[1] + im[3]
            side_re, side_im = re[1] - re[3], im[1] - im[3]
            sums = (
                (even_re + odd_re, even_im + odd_im),
                (diff_re - side_im, diff_im + side_re),
                (even_re - odd_re, even_im - odd_im),
                (diff_re + side_im, diff_im - side_re),
            )
            for rank in range(RADIX):
                a, b = sums[rank]
                if rank > 0:
                    c = twiddle_ref[rank - 1, 0, pl.ds(row, PACK)]
                    s = twiddle_ref[rank - 1, 1, pl.ds(row, PACK)]
                    a, b = a * c - b * s, a * s + b * c
                split(a, row, rank)
                split(b, quarter + row, rank)
    for pair in range(0, RADIX, 2):
        at = slice(pair * cols, (pair + 2) * cols)
        high = yhi_ref[:, at]
        value = (
            jnp.dot(hi_ref[...], high, preferred_element_type=jnp.float32)
            + jnp.dot(hi_ref[...], ylo_ref[:, at], preferred_element_type=jnp.float32)
            + jnp.dot(lo_ref[...], high, preferred_element_type=jnp.float32)
        )
        out_ref[0, pair] = value[:, :cols]
        out_ref[0, pair + 1] = value[:, cols:]

    @pl.when(plane == 0)
    def _():
        low_ref[...] = out_ref[0]

    @pl.when(plane == planes - 1)
    def _():
        high_ref[...] = out_ref[0]

    steps = quarter // SEGS
    count = slab_ref.shape[1] // (RADIX * steps)
    for seg in range(SEGS):
        for rank in range(RADIX):
            values = out_ref[0, rank, pl.ds(seg, steps, stride=SEGS)]
            slab_ref[seg, pl.ds(rank * count + plane, steps, stride=RADIX * count)] = values


def z_transform(me, sent, planes, hi, lo, twiddle):
    total, cols = sent[0].shape
    blocks = len(sent)
    quarter = hi.shape[0]
    field = (RADIX, quarter, cols)
    slabs = (SEGS, RADIX * quarter // SEGS * planes, cols)
    return pl.pallas_call(
        z_kernel,
        grid=(planes,),
        in_specs=[pl.BlockSpec(memory_space=pltpu.SMEM)]
        + [pl.BlockSpec(memory_space=pl.ANY)] * blocks
        + [
            pl.BlockSpec(hi.shape, lambda p: (0, 0)),
            pl.BlockSpec(lo.shape, lambda p: (0, 0)),
            pl.BlockSpec(twiddle.shape, lambda p: (0, 0, 0, 0)),
        ],
        out_specs=[
            pl.BlockSpec((1, *field), lambda p: (p, 0, 0, 0)),
            pl.BlockSpec(field, lambda p: (0, 0, 0)),
            pl.BlockSpec(field, lambda p: (0, 0, 0)),
            pl.BlockSpec(slabs, lambda p: (0, 0, 0)),
        ],
        out_shape=[
            jax.ShapeDtypeStruct((planes, *field), jnp.float32),
            jax.ShapeDtypeStruct(field, jnp.float32),
            jax.ShapeDtypeStruct(field, jnp.float32),
            jax.ShapeDtypeStruct(slabs, jnp.float32),
        ],
        scratch_shapes=[
            pltpu.VMEM((blocks, total, cols), jnp.int16),
            pltpu.VMEM((2 * quarter, RADIX * cols), jnp.bfloat16),
            pltpu.VMEM((2 * quarter, RADIX * cols), jnp.bfloat16),
            pltpu.SemaphoreType.DMA((blocks,)),
        ],
        cost_estimate=pl.CostEstimate(
            flops=2 * planes * quarter * 2 * quarter * RADIX * cols * 3,
            bytes_accessed=6 * 2**20,
            transcendentals=0,
        ),
        name="z_transform",
    )(me, *sent, hi, lo, twiddle)


def soft2(coeffs, value, careful):
    power = ((coeffs[3] * value + coeffs[2]) * value + coeffs[1]) * value + coeffs[0]
    grown = jnp.exp2(jnp.minimum(power, 126.0))
    soft = jnp.log2(1.0 + grown)
    if careful:
        soft = jnp.where(grown < 2.0**-12, grown * LOG2E, soft)
    return jnp.maximum(soft, power)


def render_kernel(cells, picked, coeffs_ref, index_ref, field_ref, *refs):
    edges, (out_ref, light_ref) = refs[:-2], refs[-2:]
    steps = field_ref.shape[2] // SEGS
    images = index_ref.shape[0]
    last = field_ref.shape[0] - 1
    shape = (SEGS, LANES)
    if edges:
        done_ref, before_ref, after_ref = edges
        out_ref[...] = done_ref[...]
    for plane in picked:
        here = field_ref.at[plane]
        below = before_ref if plane == 0 else field_ref.at[plane - 1]
        above = after_ref if plane == last else field_ref.at[plane + 1]

        def light(i, carry):
            rows = pl.ds(pl.multiple_of(i * SEGS, SEGS), SEGS)
            for rank in range(RADIX):
                slope = 0.5 * (above[rank, rows] - below[rank, rows])
                light_ref[rank, rows] = 1.0 + shade_gain * jnp.tanh(slope)
            return carry

        lax.fori_loop(0, steps, light, 0, unroll=2)

        def image(m, carry):
            which = index_ref[m]
            table = [
                [jnp.full(shape, coeffs_ref[which, j, n] * LOG2E, jnp.float32) for n in range(4)]
                for j in range(4)
            ]

            def step(careful, i, state):
                clear, sums = state
                rows = pl.ds(pl.multiple_of(i * SEGS, SEGS), SEGS)
                for rank in range(RADIX):
                    value = here[rank, rows]
                    depth = soft2(table[3], value, careful) * (-density / cells)
                    left = clear * jnp.exp2(depth)
                    weight = clear - left
                    if careful:
                        near = depth * (-LN2 - (0.5 * LN2 * LN2) * depth)
                        weight = jnp.where(depth > -(2.0**-9), clear * near, weight)
                    clear = left
                    weight = weight * light_ref[rank, rows]
                    sums = [
                        acc + weight * soft2(table[j], value, careful)
                        for j, acc in enumerate(sums)
                    ]
                return clear, sums

            def march(careful, unroll):
                zero = jnp.zeros(shape, jnp.float32)
                clear, sums = lax.fori_loop(
                    0,
                    steps,
                    functools.partial(step, careful),
                    (jnp.ones(shape, jnp.float32), [zero, zero, zero]),
                    unroll=unroll,
                )
                reach = clear[0:1]
                totals = [acc[0:1] for acc in sums]
                for seg in range(1, SEGS):
                    totals = [t + reach * acc[seg : seg + 1] for t, acc in zip(totals, sums)]
                    reach = reach * clear[seg : seg + 1]
                for j in range(3):
                    out_ref[m, j, plane : plane + 1] = totals[j] * LN2
                out_ref[m, 3, plane : plane + 1] = reach
                least = jnp.minimum(jnp.minimum(totals[0], totals[1]), totals[2])
                taken = 1.0 - reach
                return jnp.min(jnp.minimum(least - FAINT * taken, taken - SPARSE))

            margin = march(False, 2)

            @pl.when(jnp.logical_not(margin > 0.0))
            def _():
                march(True, 1)

            return carry

        lax.fori_loop(0, images, image, 0)


def render(cells, picked, coeffs, index, fields, *edges):
    images = index.shape[0]
    planes = fields.shape[0]
    vmem = pl.BlockSpec(memory_space=pltpu.VMEM)
    smem = pl.BlockSpec(memory_space=pltpu.SMEM)
    points = images * len(picked) * cells * LANES
    return pl.pallas_call(
        functools.partial(render_kernel, cells, picked),
        in_specs=[smem, smem, vmem] + [vmem] * len(edges),
        out_specs=vmem,
        out_shape=jax.ShapeDtypeStruct((images, 4, planes, LANES), jnp.float32),
        scratch_shapes=[pltpu.VMEM(fields.shape[1:], jnp.float32)],
        cost_estimate=pl.CostEstimate(
            flops=64 * points, bytes_accessed=4 * 2**20, transcendentals=9 * points
        ),
        name="render",
    )(coeffs, index, fields, *edges)


def shifts(axis):
    devices = lax.axis_size(axis)
    up = [(i, (i + 1) % devices) for i in range(devices)]
    return up, [(j, i) for i, j in up]


def fast_body(spectrum, transfer_coeffs, transfer_index):
    _, rows, planes, nx = spectrum.shape
    blocks = lax.axis_size("depth")
    nz = rows * blocks
    xhi, xlo = x_tables(nx, blocks)
    zhi, zlo, twiddle = z_tables(nz)
    me = lax.axis_index("depth")[None]
    modes = spectrum.reshape(2 * rows * planes, nx)
    sent = [None] * blocks
    for pair in PAIRS:
        made = x_transform(modes, me, pair, planes, xhi, xlo)
        for step, block in zip(pair, made):
            swap = [(i, i ^ step) for i in range(blocks)]
            sent[step] = lax.ppermute(block, "depth", swap) if step else block
    fields, low, high, slabs = z_transform(me, sent, planes, zhi, zlo, twiddle)
    up, down = shifts("plane")
    before = lax.ppermute(high, "plane", up)
    after = lax.ppermute(low, "plane", down)
    slabs = lax.all_to_all(
        slabs.reshape(blocks, rows, planes, LANES), "depth", split_axis=0, concat_axis=0, tiled=True
    )
    scalar_field = slabs.transpose(1, 2, 0, 3).reshape(rows, planes, nx)
    inner = tuple(range(1, planes - 1))
    picture = render(nz, inner, transfer_coeffs, transfer_index, fields)
    rendered = render(
        nz, (0, planes - 1), transfer_coeffs, transfer_index, fields, picture, before, after
    )
    return scalar_field, rendered


def with_halo(array, sides, width):
    for axis, dim in sides:
        devices, length = (lax.axis_size(axis), array.shape[dim])
        up = [(i, (i + 1) % devices) for i in range(devices)]
        down = [(j, i) for i, j in up]
        last = lax.slice_in_dim(array, length - width, length, axis=dim)
        first = lax.slice_in_dim(array, 0, width, axis=dim)
        before = lax.ppermute(last, axis, up)
        after = lax.ppermute(first, axis, down)
        array = jnp.concatenate([before, array, after], axis=dim)
    return array


def dft_tables(length):
    indices = jnp.arange(length, dtype=jnp.int32)
    phase_index = indices[:, None] * indices[None, :] % length
    angles = phase_index.astype(jnp.float32) * (2.0 * jnp.pi / length)
    scaling = 1.0 / jnp.sqrt(jnp.float32(length))
    return (jnp.cos(angles) * scaling, jnp.sin(angles) * scaling)


def polynomial(coeffs, values):
    result = coeffs[-1] + jnp.zeros_like(values)
    for degree in range(coeffs.shape[0] - 2, -1, -1):
        result = result * values + coeffs[degree]
    return result


def plane_slope(field_cells):
    padded = with_halo(field_cells, (("plane", 1),), 1)
    return 0.5 * (padded[:, 2:] - padded[:, :-2])


def render_blocks(field_cells, slope_cells, selected, blocks):
    depth_cells, plane_count, column_count = field_cells.shape
    block_cells = depth_cells // blocks
    values = field_cells.reshape(blocks, block_cells, plane_count, column_count)
    lighting = 1.0 + shade_gain * jnp.tanh(
        slope_cells.reshape(blocks, block_cells, plane_count, column_count)
    )
    per_image = []
    for which_image in range(selected.shape[0]):
        coeffs = selected[which_image]
        optical = jax.nn.softplus(polynomial(coeffs[3], values)) * (density / depth_cells)
        before = jnp.cumsum(optical, axis=1) - optical
        weight = jnp.exp(-before) * -jnp.expm1(-optical) * lighting
        block_depth = jnp.sum(optical, axis=1)
        ahead = jnp.cumsum(block_depth, axis=0) - block_depth
        reach = jnp.exp(-ahead)
        channels = []
        for channel in range(3):
            glow_cells = jax.nn.softplus(polynomial(coeffs[channel], values))
            channels.append(jnp.sum(reach * jnp.sum(weight * glow_cells, axis=1), axis=0))
        channels.append(jnp.sum(block_depth, axis=0))
        per_image.append(jnp.stack(channels))
    return jnp.stack(per_image)


def body(spectrum, transfer_coeffs, transfer_index):
    _, rows, _, nx = spectrum.shape
    cos_z, sin_z = dft_tables(rows * lax.axis_size("depth"))
    cos_x, sin_x = dft_tables(nx)
    one_hot = (
        transfer_index[:, None] == jnp.arange(transfer_coeffs.shape[0], dtype=jnp.int32)[None, :]
    ).astype(jnp.float32)
    selected = jnp.sum(one_hot[:, :, None, None] * transfer_coeffs[None], axis=1)
    depth_count = lax.axis_size("depth")
    real_part = spectrum[0].astype(jnp.float32)
    imag_part = spectrum[1].astype(jnp.float32)
    h_re = jnp.einsum("zpk,kx->zpx", real_part, cos_x, precision=highest) - jnp.einsum(
        "zpk,kx->zpx", imag_part, sin_x, precision=highest
    )
    h_im = jnp.einsum("zpk,kx->zpx", real_part, sin_x, precision=highest) + jnp.einsum(
        "zpk,kx->zpx", imag_part, cos_x, precision=highest
    )
    mixed = jnp.stack([h_re, h_im])
    arrived = lax.all_to_all(mixed, "depth", split_axis=3, concat_axis=1, tiled=True)
    field_columns = jnp.einsum("zk,kpx->zpx", cos_z, arrived[0], precision=highest) - jnp.einsum(
        "zk,kpx->zpx", sin_z, arrived[1], precision=highest
    )
    slope_cells = plane_slope(field_columns)
    merged = render_blocks(field_columns, slope_cells, selected, depth_count)
    scalar_field = lax.all_to_all(field_columns, "depth", split_axis=0, concat_axis=2, tiled=True)
    rendered = jnp.concatenate([merged[:, :3], jnp.exp(-merged[:, 3:4])], axis=1)
    return (scalar_field, rendered)


def solution(mesh):
    def pick(spectrum, *rest):
        _, rows, planes, nx = spectrum.shape
        blocks = lax.axis_size("depth")
        if nx == LANES * blocks and blocks == SEGS and planes > 2 and rows % PACK == 0:
            return fast_body(spectrum, *rest)
        return body(spectrum, *rest)

    return jax.shard_map(
        pick,
        mesh=mesh,
        in_specs=(P(None, "depth", "plane", None), P(), P()),
        out_specs=(P("depth", "plane", None), P(None, None, "plane", "depth")),
        check_vma=False,
    )
```

```python
import functools

import jax
import jax.numpy as jnp
import numpy as np
from jax import lax
from jax.experimental import pallas as pl
from jax.experimental.pallas import tpu as pltpu
from jax.sharding import PartitionSpec as P


density = 2.0
shade_gain = 0.4
highest = lax.Precision.HIGHEST
LANES = 128
SEGS = 8
RADIX = 4
PACK = 16
PAIRS = ((6, 7), (2, 4), (3, 5), (1, 0))
LEVELS = 16.0
STEPS = 32766.0
TINY = 2.0**-108
FAINT = 2.0**-9
SPARSE = 0.02
TERMS = 16
LOG2E = 1.4426950408889634
LN2 = 0.6931471805599453


def split_table(table):
    hi = table.astype(jnp.bfloat16)
    lo = (table - hi.astype(np.float64)).astype(jnp.bfloat16)
    return jnp.asarray(hi), jnp.asarray(lo)


def x_tables(nx, blocks):
    k = np.arange(nx, dtype=np.int64)
    angle = 2.0 * np.pi * ((k[:, None] * k[None, :]) % nx) / nx
    cols = nx // blocks
    cos = (np.cos(angle) / np.sqrt(nx)).reshape(nx, blocks, cols)
    sin = (np.sin(angle) / np.sqrt(nx)).reshape(nx, blocks, cols)
    return split_table(np.concatenate([cos, sin], axis=2).transpose(1, 0, 2))


def z_tables(nz):
    quarter = nz // RADIX
    q = np.arange(quarter, dtype=np.int64)
    steps = quarter // SEGS
    row = np.arange(quarter)
    m = (row % SEGS) * steps + row // SEGS
    angle = 2.0 * np.pi * ((m[:, None] * q[None, :]) % quarter) / quarter
    table = np.concatenate([np.cos(angle), -np.sin(angle)], axis=1) / np.sqrt(nz)
    turn = 2.0 * np.pi * np.arange(1, RADIX)[:, None] * q[None, :] / nz
    twiddle = np.stack([np.cos(turn), np.sin(turn)], axis=1)
    wide = np.broadcast_to(twiddle[..., None], twiddle.shape + (LANES,))
    return split_table(table) + (jnp.asarray(wide, jnp.float32),)


def level_of(peak):
    level = jnp.ceil(LEVELS * jnp.log2(jnp.maximum(peak, TINY))) + 1.0
    return level, STEPS * jnp.exp2(level * (-1.0 / LEVELS))


def code(value, scale):
    return jnp.round(value * scale).astype(jnp.int32).astype(jnp.int16)


def decode(whole, scale):
    return whole.astype(jnp.int32).astype(jnp.float32) * scale


def step_of(level):
    return jnp.exp2(level * (1.0 / LEVELS)) * (1.0 / STEPS)


def x_kernel(planes, target_ref, spec_ref, hi_ref, lo_ref, *refs):
    outs, (mixed_ref,) = refs[:-1], refs[-1:]
    half = spec_ref.shape[0] // 2
    rows = half // planes
    cols = hi_ref.shape[2] // 2
    hi = hi_ref[0]
    lo = lo_ref[0]

    def product(part):
        modes = spec_ref[part * half : (part + 1) * half]
        return jnp.dot(modes, hi, preferred_element_type=jnp.float32) + jnp.dot(
            modes, lo, preferred_element_type=jnp.float32
        )

    a = product(0)
    b = product(1)
    mixed_ref[0] = a[:, :cols] - b[:, cols:]
    mixed_ref[1] = a[:, cols:] + b[:, :cols]
    place = lax.broadcasted_iota(jnp.int32, (PACK, cols), 0)

    def emit(out_ref):
        levels = jnp.zeros((PACK, cols), jnp.float32)
        for plane in range(planes):
            parts = [mixed_ref[part, pl.ds(plane, rows, stride=planes)] for part in range(2)]
            peak = jnp.maximum(jnp.abs(parts[0]), jnp.abs(parts[1]))
            peak = jnp.max(peak, axis=0, keepdims=True)
            level, scale = level_of(peak)
            for part in range(2):
                at = (plane * 2 + part) * rows
                out_ref[at : at + rows] = code(parts[part], scale)
            levels = jnp.where(place == plane, jnp.broadcast_to(level, levels.shape), levels)
        at = planes * 2 * rows
        out_ref[at : at + PACK] = levels.astype(jnp.int32).astype(jnp.int16)

    for which, out_ref in enumerate(outs):
        pl.when(pl.program_id(0) == which)(functools.partial(emit, out_ref))


def x_transform(spec, me, pair, planes, hi, lo):
    modes, nx = spec.shape
    _, _, wide = hi.shape
    cols = wide // 2
    count = len(pair)
    sent = (modes + PACK, cols)

    def table(d, t):
        return (jnp.bitwise_xor(t[0], jnp.where(d == 0, pair[0], pair[1])), 0, 0)

    return pl.pallas_call(
        functools.partial(x_kernel, planes),
        grid_spec=pltpu.PrefetchScalarGridSpec(
            num_scalar_prefetch=1,
            grid=(count,),
            in_specs=[
                pl.BlockSpec((modes, nx), lambda d, t: (0, 0)),
                pl.BlockSpec((1, nx, wide), table),
                pl.BlockSpec((1, nx, wide), table),
            ],
            out_specs=[pl.BlockSpec(sent, lambda d, t: (0, 0))] * count,
            scratch_shapes=[pltpu.VMEM((2, modes // 2, cols), jnp.float32)],
        ),
        out_shape=[jax.ShapeDtypeStruct(sent, jnp.int16)] * count,
        cost_estimate=pl.CostEstimate(
            flops=2 * modes * nx * wide * 2 * count,
            bytes_accessed=2 * modes * nx + 4 * nx * wide * count,
            transcendentals=0,
        ),
        name="x_transform",
    )(me, spec, hi, lo)


def z_kernel(me_ref, *refs):
    blocks = SEGS
    sent, refs = refs[:blocks], refs[blocks:]
    hi_ref, lo_ref, twiddle_ref, out_ref, low_ref, high_ref, slab_ref = refs[:7]
    in_ref, yhi_ref, ylo_ref, sem = refs[7:]
    plane = pl.program_id(0)
    planes = pl.num_programs(0)
    _, total, cols = in_ref.shape
    quarter = hi_ref.shape[0]
    rows = quarter * RADIX // blocks
    per = blocks // RADIX

    @pl.when(plane == 0)
    def _():
        copies = [
            pltpu.make_async_copy(ref, in_ref.at[jnp.bitwise_xor(me_ref[0], step)], sem.at[step])
            for step, ref in enumerate(sent)
        ]
        for copy in copies:
            copy.start()
        for copy in copies:
            copy.wait()

    def split(value, row, rank):
        high = value.astype(jnp.bfloat16)
        yhi_ref[pl.ds(row, PACK), rank * cols : (rank + 1) * cols] = high
        ylo_ref[pl.ds(row, PACK), rank * cols : (rank + 1) * cols] = (
            value - high.astype(jnp.float32)
        ).astype(jnp.bfloat16)

    place = lax.broadcasted_iota(jnp.int32, (PACK, cols), 0)

    def scale_of(source):
        level = in_ref[source, total - PACK : total].astype(jnp.int32).astype(jnp.float32)
        level = jnp.sum(jnp.where(place == plane, level, 0.0), axis=0, keepdims=True)
        return step_of(level)

    base = pl.multiple_of(plane * (2 * rows), 2 * rows)
    for block in range(per):
        sources = [t * per + block for t in range(RADIX)]
        scales = [jnp.broadcast_to(scale_of(source), (PACK, cols)) for source in sources]

        def load(t, part, chunk):
            start = pl.multiple_of(base + part * rows + chunk, PACK)
            return decode(in_ref[sources[t], pl.ds(start, PACK)], scales[t])

        def turn(nth, carry):
            chunk = nth * PACK
            re = [load(t, 0, chunk) for t in range(RADIX)]
            im = [load(t, 1, chunk) for t in range(RADIX)]
            row = pl.multiple_of(block * rows + chunk, PACK)
            even_re, even_im = re[0] + re[2], im[0] + im[2]
            diff_re, diff_im = re[0] - re[2], im[0] - im[2]
            odd_re, odd_im = re[1] + re[3], im[1] + im[3]
            side_re, side_im = re[1] - re[3], im[1] - im[3]
            sums = (
                (even_re + odd_re, even_im + odd_im),
                (diff_re - side_im, diff_im + side_re),
                (even_re - odd_re, even_im - odd_im),
                (diff_re + side_im, diff_im - side_re),
            )
            for rank in range(RADIX):
                a, b = sums[rank]
                if rank > 0:
                    c = twiddle_ref[rank - 1, 0, pl.ds(row, PACK)]
                    s = twiddle_ref[rank - 1, 1, pl.ds(row, PACK)]
                    a, b = a * c - b * s, a * s + b * c
                split(a, row, rank)
                split(b, quarter + row, rank)
            return carry

        lax.fori_loop(0, rows // PACK, turn, 0, unroll=2)
    for pair in range(0, RADIX, 2):
        at = slice(pair * cols, (pair + 2) * cols)
        high = yhi_ref[:, at]
        value = (
            jnp.dot(hi_ref[...], high, preferred_element_type=jnp.float32)
            + jnp.dot(hi_ref[...], ylo_ref[:, at], preferred_element_type=jnp.float32)
            + jnp.dot(lo_ref[...], high, preferred_element_type=jnp.float32)
        )
        out_ref[0, pair] = value[:, :cols]
        out_ref[0, pair + 1] = value[:, cols:]

    def edge(edge_ref):
        peak = jnp.max(jnp.abs(out_ref[0, 0]), axis=0, keepdims=True)
        for rank in range(1, RADIX):
            peak = jnp.maximum(peak, jnp.max(jnp.abs(out_ref[0, rank]), axis=0, keepdims=True))
        level, scale = level_of(peak)
        for rank in range(RADIX):
            edge_ref[rank * quarter : (rank + 1) * quarter] = code(out_ref[0, rank], scale)
        level = jnp.broadcast_to(level, (PACK, cols)).astype(jnp.int32)
        edge_ref[RADIX * quarter :] = level.astype(jnp.int16)

    pl.when(plane == 0)(functools.partial(edge, low_ref))
    pl.when(plane == planes - 1)(functools.partial(edge, high_ref))

    steps = quarter // SEGS
    count = slab_ref.shape[1] // (RADIX * steps)
    for seg in range(SEGS):
        for rank in range(RADIX):
            values = out_ref[0, rank, pl.ds(seg, steps, stride=SEGS)]
            slab_ref[seg, pl.ds(rank * count + plane, steps, stride=RADIX * count)] = values


def z_transform(me, sent, planes, hi, lo, twiddle):
    total, cols = sent[0].shape
    blocks = len(sent)
    quarter = hi.shape[0]
    field = (RADIX, quarter, cols)
    edge = (RADIX * quarter + PACK, cols)
    slabs = (SEGS, RADIX * quarter // SEGS * planes, cols)
    return pl.pallas_call(
        z_kernel,
        grid=(planes,),
        in_specs=[pl.BlockSpec(memory_space=pltpu.SMEM)]
        + [pl.BlockSpec(memory_space=pl.ANY)] * blocks
        + [
            pl.BlockSpec(hi.shape, lambda p: (0, 0)),
            pl.BlockSpec(lo.shape, lambda p: (0, 0)),
            pl.BlockSpec(twiddle.shape, lambda p: (0, 0, 0, 0)),
        ],
        out_specs=[
            pl.BlockSpec((1, *field), lambda p: (p, 0, 0, 0)),
            pl.BlockSpec(edge, lambda p: (0, 0)),
            pl.BlockSpec(edge, lambda p: (0, 0)),
            pl.BlockSpec(slabs, lambda p: (0, 0, 0)),
        ],
        out_shape=[
            jax.ShapeDtypeStruct((planes, *field), jnp.float32),
            jax.ShapeDtypeStruct(edge, jnp.int16),
            jax.ShapeDtypeStruct(edge, jnp.int16),
            jax.ShapeDtypeStruct(slabs, jnp.float32),
        ],
        scratch_shapes=[
            pltpu.VMEM((blocks, total, cols), jnp.int16),
            pltpu.VMEM((2 * quarter, RADIX * cols), jnp.bfloat16),
            pltpu.VMEM((2 * quarter, RADIX * cols), jnp.bfloat16),
            pltpu.SemaphoreType.DMA((blocks,)),
        ],
        cost_estimate=pl.CostEstimate(
            flops=2 * planes * quarter * 2 * quarter * RADIX * cols * 3,
            bytes_accessed=6 * 2**20,
            transcendentals=0,
        ),
        name="z_transform",
    )(me, *sent, hi, lo, twiddle)


def grow(power, careful):
    grown = jnp.exp2(jnp.minimum(power, 126.0))
    soft = jnp.log2(1.0 + grown)
    if careful:
        soft = jnp.where(grown < 2.0**-12, grown * LOG2E, soft)
    return jnp.maximum(soft, power)


def cubic(coeffs, value):
    return ((coeffs[3] * value + coeffs[2]) * value + coeffs[1]) * value + coeffs[0]


def halves(value):
    high = value.astype(jnp.bfloat16).astype(jnp.float32)
    return high, (value - high).astype(jnp.bfloat16).astype(jnp.float32)


def render_kernel(cells, picked, coeffs_ref, index_ref, field_ref, *refs):
    first = len(refs) == 11
    if first:
        out_ref, table_ref, *refs = refs
    else:
        done_ref, table_ref, *halo_refs, out_ref, edge_ref = refs[:6]
        refs = refs[6:]
        before_ref, after_ref = edge_ref.at[0], edge_ref.at[1]
        out_ref[...] = done_ref[...]
    kept_ref, light_ref, lhs_ref, state_ref, sem, *refs = refs
    banks = (refs[0:2], refs[2:4])
    loads = [pltpu.make_async_copy(field_ref, kept_ref, sem.at[0])]
    if not first:
        loads.append(pltpu.make_async_copy(table_ref, lhs_ref, sem.at[1]))
    for load in loads:
        load.start()
    field_ref = kept_ref
    steps = field_ref.shape[2] // SEGS
    images = index_ref.shape[0]
    last = field_ref.shape[0] - 1
    shape = (SEGS, LANES)
    tall = 2 * SEGS
    wide = len(picked) * LANES

    def rows_of(i):
        return pl.ds(pl.multiple_of(i * SEGS, SEGS), SEGS)

    def coeffs_of(m, j):
        return [coeffs_ref[index_ref[m], j, n] * LOG2E for n in range(4)]

    lane = lax.broadcasted_iota(jnp.int32, (tall, TERMS * tall), 1)
    row = lax.broadcasted_iota(jnp.int32, (tall, TERMS * tall), 0)
    term = jnp.where(lane % tall == row, lane // tall, -1)

    def lay(m, carry):
        for j in range(4):
            splits = [halves(jnp.full((1, LANES), c, jnp.float32)) for c in coeffs_of(m, j)]
            full = jnp.full((1, LANES), coeffs_of(m, j)[0], jnp.float32)
            weights = [*splits[0], full - splits[0][0] - splits[0][1]]
            for n in range(1, 4):
                weights += [*splits[n], *splits[n]]
            tile = jnp.zeros((tall, TERMS * tall), jnp.float32)
            for at, weight in enumerate(weights):
                spread = jnp.broadcast_to(weight[:, :1], tile.shape)
                tile = jnp.where(term == at, spread, tile)
            start = pl.multiple_of((m * 4 + j) * tall, tall)
            lhs_ref[pl.ds(start, tall)] = tile.astype(jnp.bfloat16)
        return carry

    if first:
        lax.fori_loop(0, images, lay, 0)
        table_ref[...] = lhs_ref[...]
    else:
        for nth, halo_ref in enumerate(halo_refs):
            level = halo_ref[RADIX * steps * SEGS :].astype(jnp.int32).astype(jnp.float32)
            scale = step_of(level[0:1])
            for rank in range(RADIX):
                rows = slice(rank * steps * SEGS, (rank + 1) * steps * SEGS)
                edge_ref[nth, rank] = decode(halo_ref[rows], scale)
    for load in loads:
        load.wait()
    for side, plane in enumerate(picked):
        below = before_ref if plane == 0 else field_ref.at[plane - 1]
        above = after_ref if plane == last else field_ref.at[plane + 1]

        def light(i, carry):
            for rank in range(RADIX):
                slope = 0.5 * (above[rank, rows_of(i)] - below[rank, rows_of(i)])
                light_ref[side, rank, rows_of(i)] = 1.0 + shade_gain * jnp.tanh(slope)
            return carry

        lax.fori_loop(0, steps, light, 0, unroll=2)

    one = jnp.ones((tall, wide), jnp.bfloat16)

    def powers(i, bank):
        for half, poly_ref in enumerate(bank):
            value = jnp.concatenate(
                [
                    jnp.concatenate(
                        [field_ref[plane, 2 * half + odd, rows_of(i)] for plane in picked], axis=1
                    )
                    for odd in range(2)
                ],
                axis=0,
            )
            terms = [one, one, one]
            power = value
            for _ in range(3):
                high = power.astype(jnp.bfloat16)
                low = (power - high.astype(jnp.float32)).astype(jnp.bfloat16)
                terms += [high, high, low, low]
                power = power * value
            terms += [one] * (TERMS - len(terms))
            poly_ref[...] = jnp.dot(
                lhs_ref[...], jnp.concatenate(terms, axis=0), preferred_element_type=jnp.float32
            )

    def absorb(i, bank):
        for m in range(images):
            for side in range(len(picked)):
                clear = state_ref[m, side, 3]
                sums = [state_ref[m, side, j] for j in range(3)]
                for rank in range(RADIX):
                    poly_ref = bank[rank // 2]

                    def poly(j):
                        at = (m * 4 + j) * tall + (rank % 2) * SEGS
                        return poly_ref[at : at + SEGS, side * LANES : (side + 1) * LANES]

                    left = clear * jnp.exp2(grow(poly(3), False) * (-density / cells))
                    weight = (clear - left) * light_ref[side, rank, rows_of(i)]
                    clear = left
                    sums = [acc + weight * grow(poly(j), False) for j, acc in enumerate(sums)]
                state_ref[m, side, 3] = clear
                for j in range(3):
                    state_ref[m, side, j] = sums[j]

    state_ref[:, :, 0:3] = jnp.zeros((images, len(picked), 3, *shape), jnp.float32)
    state_ref[:, :, 3] = jnp.ones((images, len(picked), *shape), jnp.float32)
    powers(0, banks[0])
    powers(1, banks[1])

    def pair(k, carry):
        absorb(2 * k, banks[0])
        absorb(2 * k + 1, banks[1])
        powers(jnp.minimum(2 * k + 2, steps - 2), banks[0])
        powers(jnp.minimum(2 * k + 3, steps - 1), banks[1])
        return carry

    lax.fori_loop(0, steps // 2, pair, 0)

    seg = lax.broadcasted_iota(jnp.int32, shape, 0)

    def finish(m, plane, clear, sums):
        reach = jnp.where(seg == 0, 1.0, pltpu.roll(clear, 1, 0))
        for shift in (1, 2, 4):
            reach = reach * jnp.where(seg < shift, 1.0, pltpu.roll(reach, shift, 0))
        totals = [jnp.sum(reach * acc, axis=0, keepdims=True) for acc in sums]
        clear = (reach * clear)[SEGS - 1 :]
        for j in range(3):
            out_ref[m, j, plane : plane + 1] = totals[j] * LN2
        out_ref[m, 3, plane : plane + 1] = clear
        least = jnp.minimum(jnp.minimum(totals[0], totals[1]), totals[2])
        taken = 1.0 - clear
        return jnp.minimum(least - FAINT * taken, taken - SPARSE)

    margins = []
    for m in range(images):
        for side, plane in enumerate(picked):
            sums = [state_ref[m, side, j] for j in range(3)]
            margins.append(finish(m, plane, state_ref[m, side, 3], sums))
    while len(margins) > 1:
        margins = [
            jnp.minimum(a, b) for a, b in zip(margins[::2], margins[1::2])
        ]

    def image(m, carry):
        for side, plane in enumerate(picked):
            sums = [state_ref[m, side, j] for j in range(3)]
            margin = jnp.min(finish(m, plane, state_ref[m, side, 3], sums))

            @pl.when(jnp.logical_not(margin > 0.0))
            def _():
                table = [
                    [jnp.full(shape, c, jnp.float32) for c in coeffs_of(m, j)] for j in range(4)
                ]

                def step(i, state):
                    clear, sums = state
                    for rank in range(RADIX):
                        value = field_ref[plane, rank, rows_of(i)]
                        depth = grow(cubic(table[3], value), True) * (-density / cells)
                        left = clear * jnp.exp2(depth)
                        near = clear * depth * (-LN2 - (0.5 * LN2 * LN2) * depth)
                        weight = jnp.where(depth > -(2.0**-9), near, clear - left)
                        weight = weight * light_ref[side, rank, rows_of(i)]
                        clear = left
                        sums = [
                            acc + weight * grow(cubic(table[j], value), True)
                            for j, acc in enumerate(sums)
                        ]
                    return clear, sums

                zero = jnp.zeros(shape, jnp.float32)
                clear, sums = lax.fori_loop(
                    0, steps, step, (jnp.ones(shape, jnp.float32), [zero, zero, zero])
                )
                finish(m, plane, clear, sums)

        return carry

    @pl.when(jnp.logical_not(jnp.min(margins[0]) > 0.0))
    def _():
        lax.fori_loop(0, images, image, 0)


def render(cells, picked, coeffs, index, fields, *edges):
    images = index.shape[0]
    planes = fields.shape[0]
    vmem = pl.BlockSpec(memory_space=pltpu.VMEM)
    smem = pl.BlockSpec(memory_space=pltpu.SMEM)
    points = images * len(picked) * cells * LANES
    poly = (images * 4 * 2 * SEGS, len(picked) * LANES)
    table = (poly[0], TERMS * 2 * SEGS)
    picture = jax.ShapeDtypeStruct((images, 4, planes, LANES), jnp.float32)
    any_space = pl.BlockSpec(memory_space=pl.ANY)
    first = not edges
    return pl.pallas_call(
        functools.partial(render_kernel, cells, picked),
        in_specs=[smem, smem, any_space] + ([] if first else [vmem, any_space, vmem, vmem]),
        out_specs=[vmem, vmem] if first else vmem,
        out_shape=[picture, jax.ShapeDtypeStruct(table, jnp.bfloat16)] if first else picture,
        scratch_shapes=([] if first else [pltpu.VMEM((2, *fields.shape[1:]), jnp.float32)])
        + [
            pltpu.VMEM(fields.shape, jnp.float32),
            pltpu.VMEM((len(picked), *fields.shape[1:]), jnp.float32),
            pltpu.VMEM(table, jnp.bfloat16),
            pltpu.VMEM((images, len(picked), 4, SEGS, LANES), jnp.float32),
            pltpu.SemaphoreType.DMA((2,)),
        ]
        + [pltpu.VMEM(poly, jnp.float32)] * 4,
        cost_estimate=pl.CostEstimate(
            flops=64 * points, bytes_accessed=4 * 2**20, transcendentals=9 * points
        ),
        name="render",
    )(coeffs, index, fields, *edges)


def shifts(axis):
    devices = lax.axis_size(axis)
    up = [(i, (i + 1) % devices) for i in range(devices)]
    return up, [(j, i) for i, j in up]


def fast_body(spectrum, transfer_coeffs, transfer_index):
    _, rows, planes, nx = spectrum.shape
    blocks = lax.axis_size("depth")
    nz = rows * blocks
    xhi, xlo = x_tables(nx, blocks)
    zhi, zlo, twiddle = z_tables(nz)
    me = lax.axis_index("depth")[None]
    modes = spectrum.reshape(2 * rows * planes, nx)
    sent = [None] * blocks
    for pair in PAIRS:
        made = x_transform(modes, me, pair, planes, xhi, xlo)
        for step, block in zip(pair, made):
            swap = [(i, i ^ step) for i in range(blocks)]
            sent[step] = lax.ppermute(block, "depth", swap) if step else block
    fields, low, high, slabs = z_transform(me, sent, planes, zhi, zlo, twiddle)
    up, down = shifts("plane")
    before = lax.ppermute(high, "plane", up)
    after = lax.ppermute(low, "plane", down)
    slabs = lax.all_to_all(
        slabs.reshape(blocks, rows, planes, LANES), "depth", split_axis=0, concat_axis=0, tiled=True
    )
    scalar_field = slabs.transpose(1, 2, 0, 3).reshape(rows, planes, nx)
    inner = tuple(range(1, planes - 1))
    picture, table = render(nz, inner, transfer_coeffs, transfer_index, fields)
    rendered = render(
        nz, (0, planes - 1), transfer_coeffs, transfer_index, fields, picture, table, before, after
    )
    return scalar_field, rendered


def with_halo(array, sides, width):
    for axis, dim in sides:
        devices, length = (lax.axis_size(axis), array.shape[dim])
        up = [(i, (i + 1) % devices) for i in range(devices)]
        down = [(j, i) for i, j in up]
        last = lax.slice_in_dim(array, length - width, length, axis=dim)
        first = lax.slice_in_dim(array, 0, width, axis=dim)
        before = lax.ppermute(last, axis, up)
        after = lax.ppermute(first, axis, down)
        array = jnp.concatenate([before, array, after], axis=dim)
    return array


def dft_tables(length):
    indices = jnp.arange(length, dtype=jnp.int32)
    phase_index = indices[:, None] * indices[None, :] % length
    angles = phase_index.astype(jnp.float32) * (2.0 * jnp.pi / length)
    scaling = 1.0 / jnp.sqrt(jnp.float32(length))
    return (jnp.cos(angles) * scaling, jnp.sin(angles) * scaling)


def polynomial(coeffs, values):
    result = coeffs[-1] + jnp.zeros_like(values)
    for degree in range(coeffs.shape[0] - 2, -1, -1):
        result = result * values + coeffs[degree]
    return result


def plane_slope(field_cells):
    padded = with_halo(field_cells, (("plane", 1),), 1)
    return 0.5 * (padded[:, 2:] - padded[:, :-2])


def render_blocks(field_cells, slope_cells, selected, blocks):
    depth_cells, plane_count, column_count = field_cells.shape
    block_cells = depth_cells // blocks
    values = field_cells.reshape(blocks, block_cells, plane_count, column_count)
    lighting = 1.0 + shade_gain * jnp.tanh(
        slope_cells.reshape(blocks, block_cells, plane_count, column_count)
    )
    per_image = []
    for which_image in range(selected.shape[0]):
        coeffs = selected[which_image]
        optical = jax.nn.softplus(polynomial(coeffs[3], values)) * (density / depth_cells)
        before = jnp.cumsum(optical, axis=1) - optical
        weight = jnp.exp(-before) * -jnp.expm1(-optical) * lighting
        block_depth = jnp.sum(optical, axis=1)
        ahead = jnp.cumsum(block_depth, axis=0) - block_depth
        reach = jnp.exp(-ahead)
        channels = []
        for channel in range(3):
            glow_cells = jax.nn.softplus(polynomial(coeffs[channel], values))
            channels.append(jnp.sum(reach * jnp.sum(weight * glow_cells, axis=1), axis=0))
        channels.append(jnp.sum(block_depth, axis=0))
        per_image.append(jnp.stack(channels))
    return jnp.stack(per_image)


def body(spectrum, transfer_coeffs, transfer_index):
    _, rows, _, nx = spectrum.shape
    cos_z, sin_z = dft_tables(rows * lax.axis_size("depth"))
    cos_x, sin_x = dft_tables(nx)
    one_hot = (
        transfer_index[:, None] == jnp.arange(transfer_coeffs.shape[0], dtype=jnp.int32)[None, :]
    ).astype(jnp.float32)
    selected = jnp.sum(one_hot[:, :, None, None] * transfer_coeffs[None], axis=1)
    depth_count = lax.axis_size("depth")
    real_part = spectrum[0].astype(jnp.float32)
    imag_part = spectrum[1].astype(jnp.float32)
    h_re = jnp.einsum("zpk,kx->zpx", real_part, cos_x, precision=highest) - jnp.einsum(
        "zpk,kx->zpx", imag_part, sin_x, precision=highest
    )
    h_im = jnp.einsum("zpk,kx->zpx", real_part, sin_x, precision=highest) + jnp.einsum(
        "zpk,kx->zpx", imag_part, cos_x, precision=highest
    )
    mixed = jnp.stack([h_re, h_im])
    arrived = lax.all_to_all(mixed, "depth", split_axis=3, concat_axis=1, tiled=True)
    field_columns = jnp.einsum("zk,kpx->zpx", cos_z, arrived[0], precision=highest) - jnp.einsum(
        "zk,kpx->zpx", sin_z, arrived[1], precision=highest
    )
    slope_cells = plane_slope(field_columns)
    merged = render_blocks(field_columns, slope_cells, selected, depth_count)
    scalar_field = lax.all_to_all(field_columns, "depth", split_axis=0, concat_axis=2, tiled=True)
    rendered = jnp.concatenate([merged[:, :3], jnp.exp(-merged[:, 3:4])], axis=1)
    return (scalar_field, rendered)


def solution(mesh):
    def pick(spectrum, *rest):
        _, rows, planes, nx = spectrum.shape
        blocks = lax.axis_size("depth")
        if nx == LANES * blocks and blocks == SEGS and planes == 4 and rows % PACK == 0:
            return fast_body(spectrum, *rest)
        return body(spectrum, *rest)

    return jax.shard_map(
        pick,
        mesh=mesh,
        in_specs=(P(None, "depth", "plane", None), P(), P()),
        out_specs=(P("depth", "plane", None), P(None, None, "plane", "depth")),
        check_vma=False,
    )
```

```python
import functools

import jax
import jax.numpy as jnp
import numpy as np
from jax import lax
from jax.experimental import pallas as pl
from jax.experimental.pallas import tpu as pltpu
from jax.sharding import PartitionSpec as P


density = 2.0
shade_gain = 0.4
highest = lax.Precision.HIGHEST
LANES = 128
SEGS = 8
RADIX = 4
PACK = 16
PAIRS = ((6, 7), (2, 4), (3, 5), (1, 0))
LEVELS = 16.0
STEPS = 32766.0
TINY = 2.0**-108
FAINT = 2.0**-9
SPARSE = 0.02
TERMS = 16
VMEM_LIMIT = 24 * 2**20
LOG2E = 1.4426950408889634
LN2 = 0.6931471805599453


def split_table(table):
    hi = table.astype(jnp.bfloat16)
    lo = (table - hi.astype(np.float64)).astype(jnp.bfloat16)
    return hi, lo


def x_tables(nx, blocks):
    k = np.arange(nx, dtype=np.int64)
    angle = 2.0 * np.pi * ((k[:, None] * k[None, :]) % nx) / nx
    cols = nx // blocks
    cos = (np.cos(angle) / np.sqrt(nx)).reshape(nx, blocks, cols)
    sin = (np.sin(angle) / np.sqrt(nx)).reshape(nx, blocks, cols)
    hi, lo = split_table(np.concatenate([cos, sin], axis=2).transpose(1, 0, 2))
    return jnp.asarray(np.concatenate([hi, lo], axis=2))


def z_tables(nz):
    quarter = nz // RADIX
    q = np.arange(quarter, dtype=np.int64)
    steps = quarter // SEGS
    row = np.arange(quarter)
    m = (row % SEGS) * steps + row // SEGS
    angle = 2.0 * np.pi * ((m[:, None] * q[None, :]) % quarter) / quarter
    table = np.concatenate([np.cos(angle), -np.sin(angle)], axis=1) / np.sqrt(nz)
    turn = 2.0 * np.pi * np.arange(1, RADIX)[:, None] * q[None, :] / nz
    twiddle = np.stack([np.cos(turn), np.sin(turn)], axis=1)
    wide = np.broadcast_to(twiddle[..., None], twiddle.shape + (LANES,))
    hi, lo = split_table(table)
    return jnp.asarray(hi), jnp.asarray(lo), jnp.asarray(wide, jnp.float32)


def level_of(peak):
    level = jnp.ceil(LEVELS * jnp.log2(jnp.maximum(peak, TINY))) + 1.0
    return level, STEPS * jnp.exp2(level * (-1.0 / LEVELS))


def code(value, scale):
    return jnp.round(value * scale).astype(jnp.int32).astype(jnp.int16)


def decode(whole, scale):
    return whole.astype(jnp.int32).astype(jnp.float32) * scale


def step_of(level):
    return jnp.exp2(level * (1.0 / LEVELS)) * (1.0 / STEPS)


def x_kernel(planes, target_ref, spec_ref, table_ref, *refs):
    outs, (mixed_ref,) = refs[:-1], refs[-1:]
    half = spec_ref.shape[1] // 2
    rows = half // planes
    cols = table_ref.shape[2] // 4
    table = table_ref[0]

    def product(part):
        own = slice(part * half, (part + 1) * half)
        modes = jnp.concatenate([spec_ref[at, own] for at in range(spec_ref.shape[0])], axis=1)
        both = jnp.dot(modes, table, preferred_element_type=jnp.float32)
        return both[:, : 2 * cols] + both[:, 2 * cols :]

    a = product(0)
    b = product(1)
    mixed_ref[0] = a[:, :cols] - b[:, cols:]
    mixed_ref[1] = a[:, cols:] + b[:, :cols]
    place = lax.broadcasted_iota(jnp.int32, (PACK, cols), 0)

    def emit(out_ref):
        levels = jnp.zeros((PACK, cols), jnp.float32)
        for plane in range(planes):
            parts = [mixed_ref[part, pl.ds(plane, rows, stride=planes)] for part in range(2)]
            peak = jnp.maximum(jnp.abs(parts[0]), jnp.abs(parts[1]))
            peak = jnp.max(peak, axis=0, keepdims=True)
            level, scale = level_of(peak)
            for part in range(2):
                at = (plane * 2 + part) * rows
                out_ref[at : at + rows] = code(parts[part], scale)
            levels = jnp.where(place == plane, jnp.broadcast_to(level, levels.shape), levels)
        at = planes * 2 * rows
        out_ref[at : at + PACK] = levels.astype(jnp.int32).astype(jnp.int16)

    for which, out_ref in enumerate(outs):
        pl.when(pl.program_id(0) == which)(functools.partial(emit, out_ref))


def x_transform(spec, me, pair, planes, tables):
    tiles, modes, lanes = spec.shape
    nx = tiles * lanes
    _, _, wide = tables.shape
    cols = wide // 4
    count = len(pair)
    sent = (modes + PACK, cols)

    def table(d, t):
        return (jnp.bitwise_xor(t[0], jnp.where(d == 0, pair[0], pair[1])), 0, 0)

    return pl.pallas_call(
        functools.partial(x_kernel, planes),
        grid_spec=pltpu.PrefetchScalarGridSpec(
            num_scalar_prefetch=1,
            grid=(count,),
            in_specs=[
                pl.BlockSpec(spec.shape, lambda d, t: (0, 0, 0)),
                pl.BlockSpec((1, nx, wide), table),
            ],
            out_specs=[pl.BlockSpec(sent, lambda d, t: (0, 0))] * count,
            scratch_shapes=[pltpu.VMEM((2, modes // 2, cols), jnp.float32)],
        ),
        out_shape=[jax.ShapeDtypeStruct(sent, jnp.int16)] * count,
        cost_estimate=pl.CostEstimate(
            flops=2 * modes * nx * wide * count,
            bytes_accessed=2 * modes * nx + 2 * nx * wide * count,
            transcendentals=0,
        ),
        name="x_transform",
        compiler_params=pltpu.CompilerParams(vmem_limit_bytes=VMEM_LIMIT),
    )(me, spec, tables)


def z_kernel(me_ref, *refs):
    blocks = SEGS
    sent, refs = refs[:blocks], refs[blocks:]
    hi_ref, lo_ref, twiddle_ref, out_ref, low_ref, high_ref, slab_ref = refs[:7]
    in_ref, yhi_ref, ylo_ref, sem = refs[7:]
    plane = pl.program_id(0)
    planes = pl.num_programs(0)
    _, total, cols = in_ref.shape
    quarter = hi_ref.shape[0]
    rows = quarter * RADIX // blocks
    per = blocks // RADIX

    @pl.when(plane == 0)
    def _():
        copies = [
            pltpu.make_async_copy(ref, in_ref.at[jnp.bitwise_xor(me_ref[0], step)], sem.at[step])
            for step, ref in enumerate(sent)
        ]
        for copy in copies:
            copy.start()
        for copy in copies:
            copy.wait()

    def split(value, row, rank):
        high = value.astype(jnp.bfloat16)
        yhi_ref[pl.ds(row, PACK), rank * cols : (rank + 1) * cols] = high
        ylo_ref[pl.ds(row, PACK), rank * cols : (rank + 1) * cols] = (
            value - high.astype(jnp.float32)
        ).astype(jnp.bfloat16)

    place = lax.broadcasted_iota(jnp.int32, (PACK, cols), 0)

    def scale_of(source):
        level = in_ref[source, total - PACK : total].astype(jnp.int32).astype(jnp.float32)
        level = jnp.sum(jnp.where(place == plane, level, 0.0), axis=0, keepdims=True)
        return step_of(level)

    base = pl.multiple_of(plane * (2 * rows), 2 * rows)
    for block in range(per):
        sources = [t * per + block for t in range(RADIX)]
        scales = [jnp.broadcast_to(scale_of(source), (PACK, cols)) for source in sources]

        def load(t, part, chunk):
            start = pl.multiple_of(base + part * rows + chunk, PACK)
            return decode(in_ref[sources[t], pl.ds(start, PACK)], scales[t])

        def turn(nth, carry):
            chunk = nth * PACK
            re = [load(t, 0, chunk) for t in range(RADIX)]
            im = [load(t, 1, chunk) for t in range(RADIX)]
            row = pl.multiple_of(block * rows + chunk, PACK)
            even_re, even_im = re[0] + re[2], im[0] + im[2]
            diff_re, diff_im = re[0] - re[2], im[0] - im[2]
            odd_re, odd_im = re[1] + re[3], im[1] + im[3]
            side_re, side_im = re[1] - re[3], im[1] - im[3]
            sums = (
                (even_re + odd_re, even_im + odd_im),
                (diff_re - side_im, diff_im + side_re),
                (even_re - odd_re, even_im - odd_im),
                (diff_re + side_im, diff_im - side_re),
            )
            for rank in range(RADIX):
                a, b = sums[rank]
                if rank > 0:
                    c = twiddle_ref[rank - 1, 0, pl.ds(row, PACK)]
                    s = twiddle_ref[rank - 1, 1, pl.ds(row, PACK)]
                    a, b = a * c - b * s, a * s + b * c
                split(a, row, rank)
                split(b, quarter + row, rank)
            return carry

        lax.fori_loop(0, rows // PACK, turn, 0, unroll=2)
    for pair in range(0, RADIX, 2):
        at = slice(pair * cols, (pair + 2) * cols)
        high = yhi_ref[:, at]
        value = (
            jnp.dot(hi_ref[...], high, preferred_element_type=jnp.float32)
            + jnp.dot(hi_ref[...], ylo_ref[:, at], preferred_element_type=jnp.float32)
            + jnp.dot(lo_ref[...], high, preferred_element_type=jnp.float32)
        )
        out_ref[0, pair] = value[:, :cols]
        out_ref[0, pair + 1] = value[:, cols:]

    def edge(edge_ref):
        peak = jnp.max(jnp.abs(out_ref[0, 0]), axis=0, keepdims=True)
        for rank in range(1, RADIX):
            peak = jnp.maximum(peak, jnp.max(jnp.abs(out_ref[0, rank]), axis=0, keepdims=True))
        level, scale = level_of(peak)
        for rank in range(RADIX):
            edge_ref[rank * quarter : (rank + 1) * quarter] = code(out_ref[0, rank], scale)
        level = jnp.broadcast_to(level, (PACK, cols)).astype(jnp.int32)
        edge_ref[RADIX * quarter :] = level.astype(jnp.int16)

    pl.when(plane == 0)(functools.partial(edge, low_ref))
    pl.when(plane == planes - 1)(functools.partial(edge, high_ref))

    steps = quarter // SEGS
    count = slab_ref.shape[1] // (RADIX * steps)
    for seg in range(SEGS):
        for rank in range(RADIX):
            values = out_ref[0, rank, pl.ds(seg, steps, stride=SEGS)]
            slab_ref[seg, pl.ds(rank * count + plane, steps, stride=RADIX * count)] = values


def z_transform(me, sent, planes, hi, lo, twiddle):
    total, cols = sent[0].shape
    blocks = len(sent)
    quarter = hi.shape[0]
    field = (RADIX, quarter, cols)
    edge = (RADIX * quarter + PACK, cols)
    slabs = (SEGS, RADIX * quarter // SEGS * planes, cols)
    return pl.pallas_call(
        z_kernel,
        grid=(planes,),
        in_specs=[pl.BlockSpec(memory_space=pltpu.SMEM)]
        + [pl.BlockSpec(memory_space=pl.ANY)] * blocks
        + [
            pl.BlockSpec(hi.shape, lambda p: (0, 0)),
            pl.BlockSpec(lo.shape, lambda p: (0, 0)),
            pl.BlockSpec(twiddle.shape, lambda p: (0, 0, 0, 0)),
        ],
        out_specs=[
            pl.BlockSpec((1, *field), lambda p: (p, 0, 0, 0)),
            pl.BlockSpec(edge, lambda p: (0, 0)),
            pl.BlockSpec(edge, lambda p: (0, 0)),
            pl.BlockSpec(slabs, lambda p: (0, 0, 0)),
        ],
        out_shape=[
            jax.ShapeDtypeStruct((planes, *field), jnp.float32),
            jax.ShapeDtypeStruct(edge, jnp.int16),
            jax.ShapeDtypeStruct(edge, jnp.int16),
            jax.ShapeDtypeStruct(slabs, jnp.float32),
        ],
        scratch_shapes=[
            pltpu.VMEM((blocks, total, cols), jnp.int16),
            pltpu.VMEM((2 * quarter, RADIX * cols), jnp.bfloat16),
            pltpu.VMEM((2 * quarter, RADIX * cols), jnp.bfloat16),
            pltpu.SemaphoreType.DMA((blocks,)),
        ],
        cost_estimate=pl.CostEstimate(
            flops=2 * planes * quarter * 2 * quarter * RADIX * cols * 3,
            bytes_accessed=6 * 2**20,
            transcendentals=0,
        ),
        name="z_transform",
        compiler_params=pltpu.CompilerParams(vmem_limit_bytes=VMEM_LIMIT),
    )(me, *sent, hi, lo, twiddle)


def grow(power, careful):
    grown = jnp.exp2(jnp.minimum(power, 126.0))
    soft = jnp.log2(1.0 + grown)
    if careful:
        soft = jnp.where(grown < 2.0**-12, grown * LOG2E, soft)
    return jnp.maximum(soft, power)


def cubic(coeffs, value):
    return ((coeffs[3] * value + coeffs[2]) * value + coeffs[1]) * value + coeffs[0]


def halves(value):
    high = value.astype(jnp.bfloat16).astype(jnp.float32)
    return high, (value - high).astype(jnp.bfloat16).astype(jnp.float32)


def render_kernel(cells, picked, coeffs_ref, index_ref, field_ref, *refs):
    first = len(refs) == 11
    if first:
        out_ref, table_ref, *refs = refs
    else:
        done_ref, table_ref, *halo_refs, out_ref, edge_ref = refs[:6]
        refs = refs[6:]
        before_ref, after_ref = edge_ref.at[0], edge_ref.at[1]
        out_ref[...] = done_ref[...]
    kept_ref, light_ref, lhs_ref, state_ref, sem, *refs = refs
    banks = (refs[0:2], refs[2:4])
    loads = [pltpu.make_async_copy(field_ref, kept_ref, sem.at[0])]
    if not first:
        loads.append(pltpu.make_async_copy(table_ref, lhs_ref, sem.at[1]))
    for load in loads:
        load.start()
    field_ref = kept_ref
    steps = field_ref.shape[2] // SEGS
    images = index_ref.shape[0]
    last = field_ref.shape[0] - 1
    shape = (SEGS, LANES)
    tall = 2 * SEGS
    wide = len(picked) * LANES

    def rows_of(i):
        return pl.ds(pl.multiple_of(i * SEGS, SEGS), SEGS)

    def coeffs_of(m, j):
        return [coeffs_ref[index_ref[m], j, n] * LOG2E for n in range(4)]

    lane = lax.broadcasted_iota(jnp.int32, (tall, TERMS * tall), 1)
    row = lax.broadcasted_iota(jnp.int32, (tall, TERMS * tall), 0)
    term = jnp.where(lane % tall == row, lane // tall, -1)

    def lay(m, carry):
        for j in range(4):
            splits = [halves(jnp.full((1, LANES), c, jnp.float32)) for c in coeffs_of(m, j)]
            full = jnp.full((1, LANES), coeffs_of(m, j)[0], jnp.float32)
            weights = [*splits[0], full - splits[0][0] - splits[0][1]]
            for n in range(1, 4):
                weights += [*splits[n], *splits[n]]
            tile = jnp.zeros((tall, TERMS * tall), jnp.float32)
            for at, weight in enumerate(weights):
                spread = jnp.broadcast_to(weight[:, :1], tile.shape)
                tile = jnp.where(term == at, spread, tile)
            start = pl.multiple_of((m * 4 + j) * tall, tall)
            lhs_ref[pl.ds(start, tall)] = tile.astype(jnp.bfloat16)
        return carry

    if first:
        lax.fori_loop(0, images, lay, 0)
        table_ref[...] = lhs_ref[...]
    else:
        for nth, halo_ref in enumerate(halo_refs):
            level = halo_ref[RADIX * steps * SEGS :].astype(jnp.int32).astype(jnp.float32)
            scale = step_of(level[0:1])
            for rank in range(RADIX):
                rows = slice(rank * steps * SEGS, (rank + 1) * steps * SEGS)
                edge_ref[nth, rank] = decode(halo_ref[rows], scale)
    for load in loads:
        load.wait()
    for side, plane in enumerate(picked):
        below = before_ref if plane == 0 else field_ref.at[plane - 1]
        above = after_ref if plane == last else field_ref.at[plane + 1]

        def light(i, carry):
            for rank in range(RADIX):
                slope = 0.5 * (above[rank, rows_of(i)] - below[rank, rows_of(i)])
                light_ref[side, rank, rows_of(i)] = 1.0 + shade_gain * jnp.tanh(slope)
            return carry

        lax.fori_loop(0, steps, light, 0, unroll=2)

    one = jnp.ones((tall, wide), jnp.bfloat16)

    def powers(i, bank):
        for half, poly_ref in enumerate(bank):
            value = jnp.concatenate(
                [
                    jnp.concatenate(
                        [field_ref[plane, 2 * half + odd, rows_of(i)] for plane in picked], axis=1
                    )
                    for odd in range(2)
                ],
                axis=0,
            )
            terms = [one, one, one]
            power = value
            for _ in range(3):
                high = power.astype(jnp.bfloat16)
                low = (power - high.astype(jnp.float32)).astype(jnp.bfloat16)
                terms += [high, high, low, low]
                power = power * value
            terms += [one] * (TERMS - len(terms))
            poly_ref[...] = jnp.dot(
                lhs_ref[...], jnp.concatenate(terms, axis=0), preferred_element_type=jnp.float32
            )

    def absorb(i, bank):
        for m in range(images):
            for side in range(len(picked)):
                clear = state_ref[m, side, 3]
                sums = [state_ref[m, side, j] for j in range(3)]
                for rank in range(RADIX):
                    poly_ref = bank[rank // 2]

                    def poly(j):
                        at = (m * 4 + j) * tall + (rank % 2) * SEGS
                        return poly_ref[at : at + SEGS, side * LANES : (side + 1) * LANES]

                    left = clear * jnp.exp2(grow(poly(3), False) * (-density / cells))
                    weight = (clear - left) * light_ref[side, rank, rows_of(i)]
                    clear = left
                    sums = [acc + weight * grow(poly(j), False) for j, acc in enumerate(sums)]
                state_ref[m, side, 3] = clear
                for j in range(3):
                    state_ref[m, side, j] = sums[j]

    state_ref[:, :, 0:3] = jnp.zeros((images, len(picked), 3, *shape), jnp.float32)
    state_ref[:, :, 3] = jnp.ones((images, len(picked), *shape), jnp.float32)
    powers(0, banks[0])
    powers(1, banks[1])

    def pair(k, carry):
        absorb(2 * k, banks[0])
        absorb(2 * k + 1, banks[1])
        powers(jnp.minimum(2 * k + 2, steps - 2), banks[0])
        powers(jnp.minimum(2 * k + 3, steps - 1), banks[1])
        return carry

    lax.fori_loop(0, steps // 2, pair, 0)

    seg = lax.broadcasted_iota(jnp.int32, shape, 0)

    def finish(m, plane, clear, sums):
        reach = jnp.where(seg == 0, 1.0, pltpu.roll(clear, 1, 0))
        for shift in (1, 2, 4):
            reach = reach * jnp.where(seg < shift, 1.0, pltpu.roll(reach, shift, 0))
        totals = [jnp.sum(reach * acc, axis=0, keepdims=True) for acc in sums]
        clear = (reach * clear)[SEGS - 1 :]
        for j in range(3):
            out_ref[m, j, plane : plane + 1] = totals[j] * LN2
        out_ref[m, 3, plane : plane + 1] = clear
        least = jnp.minimum(jnp.minimum(totals[0], totals[1]), totals[2])
        taken = 1.0 - clear
        return jnp.minimum(least - FAINT * taken, taken - SPARSE)

    margins = []
    for m in range(images):
        for side, plane in enumerate(picked):
            sums = [state_ref[m, side, j] for j in range(3)]
            margins.append(finish(m, plane, state_ref[m, side, 3], sums))
    while len(margins) > 1:
        margins = [
            jnp.minimum(a, b) for a, b in zip(margins[::2], margins[1::2])
        ]

    def image(m, carry):
        for side, plane in enumerate(picked):
            sums = [state_ref[m, side, j] for j in range(3)]
            margin = jnp.min(finish(m, plane, state_ref[m, side, 3], sums))

            @pl.when(jnp.logical_not(margin > 0.0))
            def _():
                table = [
                    [jnp.full(shape, c, jnp.float32) for c in coeffs_of(m, j)] for j in range(4)
                ]

                def step(i, state):
                    clear, sums = state
                    for rank in range(RADIX):
                        value = field_ref[plane, rank, rows_of(i)]
                        depth = grow(cubic(table[3], value), True) * (-density / cells)
                        left = clear * jnp.exp2(depth)
                        near = clear * depth * (-LN2 - (0.5 * LN2 * LN2) * depth)
                        weight = jnp.where(depth > -(2.0**-9), near, clear - left)
                        weight = weight * light_ref[side, rank, rows_of(i)]
                        clear = left
                        sums = [
                            acc + weight * grow(cubic(table[j], value), True)
                            for j, acc in enumerate(sums)
                        ]
                    return clear, sums

                zero = jnp.zeros(shape, jnp.float32)
                clear, sums = lax.fori_loop(
                    0, steps, step, (jnp.ones(shape, jnp.float32), [zero, zero, zero])
                )
                finish(m, plane, clear, sums)

        return carry

    @pl.when(jnp.logical_not(jnp.min(margins[0]) > 0.0))
    def _():
        lax.fori_loop(0, images, image, 0)


def render(cells, picked, coeffs, index, fields, *edges):
    images = index.shape[0]
    planes = fields.shape[0]
    vmem = pl.BlockSpec(memory_space=pltpu.VMEM)
    smem = pl.BlockSpec(memory_space=pltpu.SMEM)
    points = images * len(picked) * cells * LANES
    poly = (images * 4 * 2 * SEGS, len(picked) * LANES)
    table = (poly[0], TERMS * 2 * SEGS)
    picture = jax.ShapeDtypeStruct((images, 4, planes, LANES), jnp.float32)
    any_space = pl.BlockSpec(memory_space=pl.ANY)
    first = not edges
    return pl.pallas_call(
        functools.partial(render_kernel, cells, picked),
        in_specs=[smem, smem, any_space] + ([] if first else [vmem, any_space, vmem, vmem]),
        out_specs=[vmem, vmem] if first else vmem,
        out_shape=[picture, jax.ShapeDtypeStruct(table, jnp.bfloat16)] if first else picture,
        scratch_shapes=([] if first else [pltpu.VMEM((2, *fields.shape[1:]), jnp.float32)])
        + [
            pltpu.VMEM(fields.shape, jnp.float32),
            pltpu.VMEM((len(picked), *fields.shape[1:]), jnp.float32),
            pltpu.VMEM(table, jnp.bfloat16),
            pltpu.VMEM((images, len(picked), 4, SEGS, LANES), jnp.float32),
            pltpu.SemaphoreType.DMA((2,)),
        ]
        + [pltpu.VMEM(poly, jnp.float32)] * 4,
        cost_estimate=pl.CostEstimate(
            flops=64 * points, bytes_accessed=4 * 2**20, transcendentals=9 * points
        ),
        name="render",
        compiler_params=pltpu.CompilerParams(vmem_limit_bytes=VMEM_LIMIT),
    )(coeffs, index, fields, *edges)


def shifts(axis):
    devices = lax.axis_size(axis)
    up = [(i, (i + 1) % devices) for i in range(devices)]
    return up, [(j, i) for i, j in up]


def fast_body(spectrum, transfer_coeffs, transfer_index):
    _, rows, planes, nx = spectrum.shape
    blocks = lax.axis_size("depth")
    nz = rows * blocks
    x_table = x_tables(nx, blocks)
    zhi, zlo, twiddle = z_tables(nz)
    me = lax.axis_index("depth")[None]
    modes = spectrum.reshape(2 * rows * planes, blocks, LANES).transpose(1, 0, 2)
    sent = [None] * blocks
    for pair in PAIRS:
        made = x_transform(modes, me, pair, planes, x_table)
        for step, block in zip(pair, made):
            swap = [(i, i ^ step) for i in range(blocks)]
            sent[step] = lax.ppermute(block, "depth", swap) if step else block
    fields, low, high, slabs = z_transform(me, sent, planes, zhi, zlo, twiddle)
    up, down = shifts("plane")
    before = lax.ppermute(high, "plane", up)
    after = lax.ppermute(low, "plane", down)
    slabs = lax.all_to_all(
        slabs.reshape(blocks, rows, planes, LANES), "depth", split_axis=0, concat_axis=0, tiled=True
    )
    scalar_field = slabs.transpose(1, 2, 0, 3).reshape(rows, planes, nx)
    inner = tuple(range(1, planes - 1))
    picture, table = render(nz, inner, transfer_coeffs, transfer_index, fields)
    rendered = render(
        nz, (0, planes - 1), transfer_coeffs, transfer_index, fields, picture, table, before, after
    )
    return scalar_field, rendered


def with_halo(array, sides, width):
    for axis, dim in sides:
        devices, length = (lax.axis_size(axis), array.shape[dim])
        up = [(i, (i + 1) % devices) for i in range(devices)]
        down = [(j, i) for i, j in up]
        last = lax.slice_in_dim(array, length - width, length, axis=dim)
        first = lax.slice_in_dim(array, 0, width, axis=dim)
        before = lax.ppermute(last, axis, up)
        after = lax.ppermute(first, axis, down)
        array = jnp.concatenate([before, array, after], axis=dim)
    return array


def dft_tables(length):
    indices = jnp.arange(length, dtype=jnp.int32)
    phase_index = indices[:, None] * indices[None, :] % length
    angles = phase_index.astype(jnp.float32) * (2.0 * jnp.pi / length)
    scaling = 1.0 / jnp.sqrt(jnp.float32(length))
    return (jnp.cos(angles) * scaling, jnp.sin(angles) * scaling)


def polynomial(coeffs, values):
    result = coeffs[-1] + jnp.zeros_like(values)
    for degree in range(coeffs.shape[0] - 2, -1, -1):
        result = result * values + coeffs[degree]
    return result


def plane_slope(field_cells):
    padded = with_halo(field_cells, (("plane", 1),), 1)
    return 0.5 * (padded[:, 2:] - padded[:, :-2])


def render_blocks(field_cells, slope_cells, selected, blocks):
    depth_cells, plane_count, column_count = field_cells.shape
    block_cells = depth_cells // blocks
    values = field_cells.reshape(blocks, block_cells, plane_count, column_count)
    lighting = 1.0 + shade_gain * jnp.tanh(
        slope_cells.reshape(blocks, block_cells, plane_count, column_count)
    )
    per_image = []
    for which_image in range(selected.shape[0]):
        coeffs = selected[which_image]
        optical = jax.nn.softplus(polynomial(coeffs[3], values)) * (density / depth_cells)
        before = jnp.cumsum(optical, axis=1) - optical
        weight = jnp.exp(-before) * -jnp.expm1(-optical) * lighting
        block_depth = jnp.sum(optical, axis=1)
        ahead = jnp.cumsum(block_depth, axis=0) - block_depth
        reach = jnp.exp(-ahead)
        channels = []
        for channel in range(3):
            glow_cells = jax.nn.softplus(polynomial(coeffs[channel], values))
            channels.append(jnp.sum(reach * jnp.sum(weight * glow_cells, axis=1), axis=0))
        channels.append(jnp.sum(block_depth, axis=0))
        per_image.append(jnp.stack(channels))
    return jnp.stack(per_image)


def body(spectrum, transfer_coeffs, transfer_index):
    _, rows, _, nx = spectrum.shape
    cos_z, sin_z = dft_tables(rows * lax.axis_size("depth"))
    cos_x, sin_x = dft_tables(nx)
    one_hot = (
        transfer_index[:, None] == jnp.arange(transfer_coeffs.shape[0], dtype=jnp.int32)[None, :]
    ).astype(jnp.float32)
    selected = jnp.sum(one_hot[:, :, None, None] * transfer_coeffs[None], axis=1)
    depth_count = lax.axis_size("depth")
    real_part = spectrum[0].astype(jnp.float32)
    imag_part = spectrum[1].astype(jnp.float32)
    h_re = jnp.einsum("zpk,kx->zpx", real_part, cos_x, precision=highest) - jnp.einsum(
        "zpk,kx->zpx", imag_part, sin_x, precision=highest
    )
    h_im = jnp.einsum("zpk,kx->zpx", real_part, sin_x, precision=highest) + jnp.einsum(
        "zpk,kx->zpx", imag_part, cos_x, precision=highest
    )
    mixed = jnp.stack([h_re, h_im])
    arrived = lax.all_to_all(mixed, "depth", split_axis=3, concat_axis=1, tiled=True)
    field_columns = jnp.einsum("zk,kpx->zpx", cos_z, arrived[0], precision=highest) - jnp.einsum(
        "zk,kpx->zpx", sin_z, arrived[1], precision=highest
    )
    slope_cells = plane_slope(field_columns)
    merged = render_blocks(field_columns, slope_cells, selected, depth_count)
    scalar_field = lax.all_to_all(field_columns, "depth", split_axis=0, concat_axis=2, tiled=True)
    rendered = jnp.concatenate([merged[:, :3], jnp.exp(-merged[:, 3:4])], axis=1)
    return (scalar_field, rendered)


def solution(mesh):
    def pick(spectrum, *rest):
        _, rows, planes, nx = spectrum.shape
        blocks = lax.axis_size("depth")
        if nx == LANES * blocks and blocks == SEGS and planes == 4 and rows % PACK == 0:
            return fast_body(spectrum, *rest)
        return body(spectrum, *rest)

    return jax.shard_map(
        pick,
        mesh=mesh,
        in_specs=(P(None, "depth", "plane", None), P(), P()),
        out_specs=(P("depth", "plane", None), P(None, None, "plane", "depth")),
        check_vma=False,
    )
```

```python
import functools

import jax
import jax.numpy as jnp
import numpy as np
from jax import lax
from jax.experimental import pallas as pl
from jax.experimental.pallas import tpu as pltpu
from jax.sharding import PartitionSpec as P


density = 2.0
shade_gain = 0.4
highest = lax.Precision.HIGHEST
LANES = 128
SEGS = 8
RADIX = 4
PACK = 16
PAIRS = ((6, 7), (2, 4), (3, 5), (1, 0))
LEVELS = 16.0
STEPS = 32766.0
TINY = 2.0**-108
FAINT = 2.0**-9
SPARSE = 0.02
TERMS = 16
VMEM_LIMIT = 14 * 2**20
RENDER_LIMIT = 14 * 2**20
LOG2E = 1.4426950408889634
LN2 = 0.6931471805599453


def split_table(table):
    hi = table.astype(jnp.bfloat16)
    lo = (table - hi.astype(np.float64)).astype(jnp.bfloat16)
    return hi, lo


def x_tables(nx, blocks):
    k = np.arange(nx, dtype=np.int64)
    angle = 2.0 * np.pi * ((k[:, None] * k[None, :]) % nx) / nx
    cols = nx // blocks
    cos = (np.cos(angle) / np.sqrt(nx)).reshape(nx, blocks, cols)
    sin = (np.sin(angle) / np.sqrt(nx)).reshape(nx, blocks, cols)
    hi, lo = split_table(np.concatenate([cos, sin], axis=2).transpose(1, 0, 2))
    return jnp.asarray(np.concatenate([hi, lo], axis=2)[: blocks // RADIX])


def z_tables(nz):
    quarter = nz // RADIX
    q = np.arange(quarter, dtype=np.int64)
    steps = quarter // SEGS
    row = np.arange(quarter)
    m = (row % SEGS) * steps + row // SEGS
    angle = 2.0 * np.pi * ((m[:, None] * q[None, :]) % quarter) / quarter
    table = np.concatenate([np.cos(angle), -np.sin(angle)], axis=1) / np.sqrt(nz)
    turn = 2.0 * np.pi * np.arange(1, RADIX)[:, None] * q[None, :] / nz
    twiddle = np.stack([np.cos(turn), np.sin(turn)], axis=1)
    wide = np.broadcast_to(twiddle[..., None], twiddle.shape + (LANES,))
    hi, lo = split_table(table)
    return jnp.asarray(hi), jnp.asarray(lo), jnp.asarray(wide, jnp.float32)


def level_of(peak):
    level = jnp.ceil(LEVELS * jnp.log2(jnp.maximum(peak, TINY))) + 1.0
    return level, STEPS * jnp.exp2(level * (-1.0 / LEVELS))


def code(value, scale):
    return jnp.round(value * scale).astype(jnp.int32).astype(jnp.int16)


def decode(whole, scale):
    return whole.astype(jnp.int32).astype(jnp.float32) * scale


def step_of(level):
    return jnp.exp2(level * (1.0 / LEVELS)) * (1.0 / STEPS)


def x_kernel(planes, blocks, pair, target_ref, spec_ref, table_ref, *refs):
    outs, (mixed_ref,) = refs[:-1], refs[-1:]
    half = spec_ref.shape[1] // 2
    rows = half // planes
    cols = table_ref.shape[2] // 4
    step = jnp.where(pl.program_id(0) == 0, pair[0], pair[1])
    turns = jnp.bitwise_xor(target_ref[0], step) // (blocks // RADIX)
    row = lax.broadcasted_iota(jnp.int32, (PACK, cols), 0)
    phase = (row % RADIX * turns) % RADIX
    cosine = jnp.where(phase == 0, 1.0, jnp.where(phase == 2, -1.0, 0.0)).astype(jnp.bfloat16)
    sine = jnp.where(phase == 1, 1.0, jnp.where(phase == 3, -1.0, 0.0)).astype(jnp.bfloat16)

    def turned(at):
        parts = [
            table_ref[0, at : at + PACK, part * cols : (part + 1) * cols] for part in range(4)
        ]
        made = []
        for c, s in (parts[:2], parts[2:]):
            made += [c * cosine - s * sine, c * sine + s * cosine]
        return jnp.concatenate(made, axis=1)

    table = jnp.concatenate([turned(at) for at in range(0, table_ref.shape[1], PACK)], axis=0)

    def product(part):
        own = slice(part * half, (part + 1) * half)
        modes = jnp.concatenate([spec_ref[at, own] for at in range(spec_ref.shape[0])], axis=1)
        both = jnp.dot(modes, table, preferred_element_type=jnp.float32)
        return both[:, : 2 * cols] + both[:, 2 * cols :]

    a = product(0)
    b = product(1)
    mixed_ref[0] = a[:, :cols] - b[:, cols:]
    mixed_ref[1] = a[:, cols:] + b[:, :cols]
    place = lax.broadcasted_iota(jnp.int32, (PACK, cols), 0)

    def emit(out_ref):
        levels = jnp.zeros((PACK, cols), jnp.float32)
        for plane in range(planes):
            parts = [mixed_ref[part, pl.ds(plane, rows, stride=planes)] for part in range(2)]
            peak = jnp.maximum(jnp.abs(parts[0]), jnp.abs(parts[1]))
            peak = jnp.max(peak, axis=0, keepdims=True)
            level, scale = level_of(peak)
            for part in range(2):
                at = (plane * 2 + part) * rows
                out_ref[at : at + rows] = code(parts[part], scale)
            levels = jnp.where(place == plane, jnp.broadcast_to(level, levels.shape), levels)
        at = planes * 2 * rows
        out_ref[at : at + PACK] = levels.astype(jnp.int32).astype(jnp.int16)

    for which, out_ref in enumerate(outs):
        pl.when(pl.program_id(0) == which)(functools.partial(emit, out_ref))


def x_transform(spec, me, pair, planes, tables):
    tiles, modes, lanes = spec.shape
    nx = tiles * lanes
    _, _, wide = tables.shape
    cols = wide // 4
    count = len(pair)
    sent = (modes + PACK, cols)

    def table(d, t):
        return (jnp.bitwise_xor(t[0], jnp.where(d == 0, pair[0], pair[1])) % (tiles // RADIX), 0, 0)

    return pl.pallas_call(
        functools.partial(x_kernel, planes, tiles, pair),
        grid_spec=pltpu.PrefetchScalarGridSpec(
            num_scalar_prefetch=1,
            grid=(count,),
            in_specs=[
                pl.BlockSpec(spec.shape, lambda d, t: (0, 0, 0)),
                pl.BlockSpec((1, nx, wide), table),
            ],
            out_specs=[pl.BlockSpec(sent, lambda d, t: (0, 0))] * count,
            scratch_shapes=[pltpu.VMEM((2, modes // 2, cols), jnp.float32)],
        ),
        out_shape=[jax.ShapeDtypeStruct(sent, jnp.int16)] * count,
        cost_estimate=pl.CostEstimate(
            flops=2 * modes * nx * wide * count,
            bytes_accessed=2 * modes * nx + 2 * nx * wide * count,
            transcendentals=0,
        ),
        name="x_transform",
        compiler_params=pltpu.CompilerParams(vmem_limit_bytes=VMEM_LIMIT),
    )(me, spec, tables)


def z_kernel(me_ref, *refs):
    blocks = SEGS
    sent, refs = refs[:blocks], refs[blocks:]
    hi_ref, lo_ref, twiddle_ref, out_ref, low_ref, high_ref, slab_ref = refs[:7]
    in_ref, yhi_ref, ylo_ref, sem = refs[7:]
    plane = pl.program_id(0)
    planes = pl.num_programs(0)
    _, total, cols = in_ref.shape
    quarter = hi_ref.shape[0]
    rows = quarter * RADIX // blocks
    per = blocks // RADIX

    @pl.when(plane == 0)
    def _():
        copies = [
            pltpu.make_async_copy(ref, in_ref.at[jnp.bitwise_xor(me_ref[0], step)], sem.at[step])
            for step, ref in enumerate(sent)
        ]
        for copy in copies:
            copy.start()
        for copy in copies:
            copy.wait()

    def split(value, row, rank):
        high = value.astype(jnp.bfloat16)
        yhi_ref[pl.ds(row, PACK), rank * cols : (rank + 1) * cols] = high
        ylo_ref[pl.ds(row, PACK), rank * cols : (rank + 1) * cols] = (
            value - high.astype(jnp.float32)
        ).astype(jnp.bfloat16)

    place = lax.broadcasted_iota(jnp.int32, (PACK, cols), 0)

    def scale_of(source):
        level = in_ref[source, total - PACK : total].astype(jnp.int32).astype(jnp.float32)
        level = jnp.sum(jnp.where(place == plane, level, 0.0), axis=0, keepdims=True)
        return step_of(level)

    base = pl.multiple_of(plane * (2 * rows), 2 * rows)
    for block in range(per):
        sources = [t * per + block for t in range(RADIX)]
        scales = [jnp.broadcast_to(scale_of(source), (PACK, cols)) for source in sources]

        def load(t, part, chunk):
            start = pl.multiple_of(base + part * rows + chunk, PACK)
            return decode(in_ref[sources[t], pl.ds(start, PACK)], scales[t])

        def turn(nth, carry):
            chunk = nth * PACK
            re = [load(t, 0, chunk) for t in range(RADIX)]
            im = [load(t, 1, chunk) for t in range(RADIX)]
            row = pl.multiple_of(block * rows + chunk, PACK)
            even_re, even_im = re[0] + re[2], im[0] + im[2]
            diff_re, diff_im = re[0] - re[2], im[0] - im[2]
            odd_re, odd_im = re[1] + re[3], im[1] + im[3]
            side_re, side_im = re[1] - re[3], im[1] - im[3]
            sums = (
                (even_re + odd_re, even_im + odd_im),
                (diff_re - side_im, diff_im + side_re),
                (even_re - odd_re, even_im - odd_im),
                (diff_re + side_im, diff_im - side_re),
            )
            for rank in range(RADIX):
                a, b = sums[rank]
                if rank > 0:
                    c = twiddle_ref[rank - 1, 0, pl.ds(row, PACK)]
                    s = twiddle_ref[rank - 1, 1, pl.ds(row, PACK)]
                    a, b = a * c - b * s, a * s + b * c
                split(a, row, rank)
                split(b, quarter + row, rank)
            return carry

        lax.fori_loop(0, rows // PACK, turn, 0, unroll=2)
    for pair in range(0, RADIX, 2):
        at = slice(pair * cols, (pair + 2) * cols)
        high = yhi_ref[:, at]
        value = (
            jnp.dot(hi_ref[...], high, preferred_element_type=jnp.float32)
            + jnp.dot(hi_ref[...], ylo_ref[:, at], preferred_element_type=jnp.float32)
            + jnp.dot(lo_ref[...], high, preferred_element_type=jnp.float32)
        )
        out_ref[0, pair] = value[:, :cols]
        out_ref[0, pair + 1] = value[:, cols:]

    def edge(edge_ref):
        peak = jnp.max(jnp.abs(out_ref[0, 0]), axis=0, keepdims=True)
        for rank in range(1, RADIX):
            peak = jnp.maximum(peak, jnp.max(jnp.abs(out_ref[0, rank]), axis=0, keepdims=True))
        level, scale = level_of(peak)
        for rank in range(RADIX):
            edge_ref[rank * quarter : (rank + 1) * quarter] = code(out_ref[0, rank], scale)
        level = jnp.broadcast_to(level, (PACK, cols)).astype(jnp.int32)
        edge_ref[RADIX * quarter :] = level.astype(jnp.int16)

    pl.when(plane == 0)(functools.partial(edge, low_ref))
    pl.when(plane == planes - 1)(functools.partial(edge, high_ref))

    steps = quarter // SEGS
    count = slab_ref.shape[1] // (RADIX * steps)
    for seg in range(SEGS):
        for rank in range(RADIX):
            values = out_ref[0, rank, pl.ds(seg, steps, stride=SEGS)]
            slab_ref[seg, pl.ds(rank * count + plane, steps, stride=RADIX * count)] = values


def z_transform(me, sent, planes, hi, lo, twiddle):
    total, cols = sent[0].shape
    blocks = len(sent)
    quarter = hi.shape[0]
    field = (RADIX, quarter, cols)
    edge = (RADIX * quarter + PACK, cols)
    slabs = (SEGS, RADIX * quarter // SEGS * planes, cols)
    return pl.pallas_call(
        z_kernel,
        grid=(planes,),
        in_specs=[pl.BlockSpec(memory_space=pltpu.SMEM)]
        + [pl.BlockSpec(memory_space=pl.ANY)] * blocks
        + [
            pl.BlockSpec(hi.shape, lambda p: (0, 0)),
            pl.BlockSpec(lo.shape, lambda p: (0, 0)),
            pl.BlockSpec(twiddle.shape, lambda p: (0, 0, 0, 0)),
        ],
        out_specs=[
            pl.BlockSpec((1, *field), lambda p: (p, 0, 0, 0)),
            pl.BlockSpec(edge, lambda p: (0, 0)),
            pl.BlockSpec(edge, lambda p: (0, 0)),
            pl.BlockSpec(slabs, lambda p: (0, 0, 0)),
        ],
        out_shape=[
            jax.ShapeDtypeStruct((planes, *field), jnp.float32),
            jax.ShapeDtypeStruct(edge, jnp.int16),
            jax.ShapeDtypeStruct(edge, jnp.int16),
            jax.ShapeDtypeStruct(slabs, jnp.float32),
        ],
        scratch_shapes=[
            pltpu.VMEM((blocks, total, cols), jnp.int16),
            pltpu.VMEM((2 * quarter, RADIX * cols), jnp.bfloat16),
            pltpu.VMEM((2 * quarter, RADIX * cols), jnp.bfloat16),
            pltpu.SemaphoreType.DMA((blocks,)),
        ],
        cost_estimate=pl.CostEstimate(
            flops=2 * planes * quarter * 2 * quarter * RADIX * cols * 3,
            bytes_accessed=6 * 2**20,
            transcendentals=0,
        ),
        name="z_transform",
        compiler_params=pltpu.CompilerParams(vmem_limit_bytes=VMEM_LIMIT),
    )(me, *sent, hi, lo, twiddle)


def grow(power, careful):
    grown = jnp.exp2(jnp.minimum(power, 126.0))
    soft = jnp.log2(1.0 + grown)
    if careful:
        soft = jnp.where(grown < 2.0**-12, grown * LOG2E, soft)
    return jnp.maximum(soft, power)


def cubic(coeffs, value):
    return ((coeffs[3] * value + coeffs[2]) * value + coeffs[1]) * value + coeffs[0]


def halves(value):
    high = value.astype(jnp.bfloat16).astype(jnp.float32)
    return high, (value - high).astype(jnp.bfloat16).astype(jnp.float32)


def render_kernel(cells, picked, coeffs_ref, index_ref, field_ref, *refs):
    first = len(refs) == 11
    if first:
        out_ref, table_ref, *refs = refs
    else:
        done_ref, table_ref, *halo_refs, out_ref, edge_ref = refs[:6]
        refs = refs[6:]
        before_ref, after_ref = edge_ref.at[0], edge_ref.at[1]
        out_ref[...] = done_ref[...]
    kept_ref, light_ref, lhs_ref, state_ref, sem, *refs = refs
    banks = (refs[0:2], refs[2:4])
    loads = [pltpu.make_async_copy(field_ref, kept_ref, sem.at[0])]
    if not first:
        loads.append(pltpu.make_async_copy(table_ref, lhs_ref, sem.at[1]))
    for load in loads:
        load.start()
    field_ref = kept_ref
    steps = field_ref.shape[2] // SEGS
    images = index_ref.shape[0]
    last = field_ref.shape[0] - 1
    shape = (SEGS, LANES)
    tall = 2 * SEGS
    wide = len(picked) * LANES

    def rows_of(i):
        return pl.ds(pl.multiple_of(i * SEGS, SEGS), SEGS)

    def coeffs_of(m, j):
        return [coeffs_ref[index_ref[m], j, n] * LOG2E for n in range(4)]

    lane = lax.broadcasted_iota(jnp.int32, (tall, TERMS * tall), 1)
    row = lax.broadcasted_iota(jnp.int32, (tall, TERMS * tall), 0)
    term = jnp.where(lane % tall == row, lane // tall, -1)

    def lay(m, carry):
        for j in range(4):
            splits = [halves(jnp.full((1, LANES), c, jnp.float32)) for c in coeffs_of(m, j)]
            full = jnp.full((1, LANES), coeffs_of(m, j)[0], jnp.float32)
            weights = [*splits[0], full - splits[0][0] - splits[0][1]]
            for n in range(1, 4):
                weights += [*splits[n], *splits[n]]
            tile = jnp.zeros((tall, TERMS * tall), jnp.float32)
            for at, weight in enumerate(weights):
                spread = jnp.broadcast_to(weight[:, :1], tile.shape)
                tile = jnp.where(term == at, spread, tile)
            start = pl.multiple_of((m * 4 + j) * tall, tall)
            lhs_ref[pl.ds(start, tall)] = tile.astype(jnp.bfloat16)
        return carry

    if first:
        lax.fori_loop(0, images, lay, 0)
        table_ref[...] = lhs_ref[...]
    else:
        for nth, halo_ref in enumerate(halo_refs):
            level = halo_ref[RADIX * steps * SEGS :].astype(jnp.int32).astype(jnp.float32)
            scale = step_of(level[0:1])
            for rank in range(RADIX):
                rows = slice(rank * steps * SEGS, (rank + 1) * steps * SEGS)
                edge_ref[nth, rank] = decode(halo_ref[rows], scale)
    for load in loads:
        load.wait()
    for side, plane in enumerate(picked):
        below = before_ref if plane == 0 else field_ref.at[plane - 1]
        above = after_ref if plane == last else field_ref.at[plane + 1]

        def light(i, carry):
            for rank in range(RADIX):
                slope = 0.5 * (above[rank, rows_of(i)] - below[rank, rows_of(i)])
                light_ref[side, rank, rows_of(i)] = 1.0 + shade_gain * jnp.tanh(slope)
            return carry

        lax.fori_loop(0, steps, light, 0, unroll=2)

    one = jnp.ones((tall, wide), jnp.bfloat16)

    def powers(i, bank):
        for half, poly_ref in enumerate(bank):
            value = jnp.concatenate(
                [
                    jnp.concatenate(
                        [field_ref[plane, 2 * half + odd, rows_of(i)] for plane in picked], axis=1
                    )
                    for odd in range(2)
                ],
                axis=0,
            )
            terms = [one, one, one]
            power = value
            for _ in range(3):
                high = power.astype(jnp.bfloat16)
                low = (power - high.astype(jnp.float32)).astype(jnp.bfloat16)
                terms += [high, high, low, low]
                power = power * value
            terms += [one] * (TERMS - len(terms))
            poly_ref[...] = jnp.dot(
                lhs_ref[...], jnp.concatenate(terms, axis=0), preferred_element_type=jnp.float32
            )

    def absorb(i, bank):
        for m in range(images):
            for side in range(len(picked)):
                clear = state_ref[m, side, 3]
                sums = [state_ref[m, side, j] for j in range(3)]
                for rank in range(RADIX):
                    poly_ref = bank[rank // 2]

                    def poly(j):
                        at = (m * 4 + j) * tall + (rank % 2) * SEGS
                        return poly_ref[at : at + SEGS, side * LANES : (side + 1) * LANES]

                    left = clear * jnp.exp2(grow(poly(3), False) * (-density / cells))
                    weight = (clear - left) * light_ref[side, rank, rows_of(i)]
                    clear = left
                    sums = [acc + weight * grow(poly(j), False) for j, acc in enumerate(sums)]
                state_ref[m, side, 3] = clear
                for j in range(3):
                    state_ref[m, side, j] = sums[j]

    state_ref[:, :, 0:3] = jnp.zeros((images, len(picked), 3, *shape), jnp.float32)
    state_ref[:, :, 3] = jnp.ones((images, len(picked), *shape), jnp.float32)
    powers(0, banks[0])
    powers(1, banks[1])

    def pair(k, carry):
        absorb(2 * k, banks[0])
        absorb(2 * k + 1, banks[1])
        powers(jnp.minimum(2 * k + 2, steps - 2), banks[0])
        powers(jnp.minimum(2 * k + 3, steps - 1), banks[1])
        return carry

    lax.fori_loop(0, steps // 2, pair, 0)

    seg = lax.broadcasted_iota(jnp.int32, shape, 0)

    def finish(m, plane, clear, sums):
        reach = jnp.where(seg == 0, 1.0, pltpu.roll(clear, 1, 0))
        for shift in (1, 2, 4):
            reach = reach * jnp.where(seg < shift, 1.0, pltpu.roll(reach, shift, 0))
        totals = [jnp.sum(reach * acc, axis=0, keepdims=True) for acc in sums]
        clear = (reach * clear)[SEGS - 1 :]
        for j in range(3):
            out_ref[m, j, plane : plane + 1] = totals[j] * LN2
        out_ref[m, 3, plane : plane + 1] = clear
        least = jnp.minimum(jnp.minimum(totals[0], totals[1]), totals[2])
        taken = 1.0 - clear
        return jnp.minimum(least - FAINT * taken, taken - SPARSE)

    margins = []
    for m in range(images):
        for side, plane in enumerate(picked):
            sums = [state_ref[m, side, j] for j in range(3)]
            margins.append(finish(m, plane, state_ref[m, side, 3], sums))
    while len(margins) > 1:
        margins = [
            jnp.minimum(a, b) for a, b in zip(margins[::2], margins[1::2])
        ]

    def image(m, carry):
        for side, plane in enumerate(picked):
            sums = [state_ref[m, side, j] for j in range(3)]
            margin = jnp.min(finish(m, plane, state_ref[m, side, 3], sums))

            @pl.when(jnp.logical_not(margin > 0.0))
            def _():
                table = [
                    [jnp.full(shape, c, jnp.float32) for c in coeffs_of(m, j)] for j in range(4)
                ]

                def step(i, state):
                    clear, sums = state
                    for rank in range(RADIX):
                        value = field_ref[plane, rank, rows_of(i)]
                        depth = grow(cubic(table[3], value), True) * (-density / cells)
                        left = clear * jnp.exp2(depth)
                        near = clear * depth * (-LN2 - (0.5 * LN2 * LN2) * depth)
                        weight = jnp.where(depth > -(2.0**-9), near, clear - left)
                        weight = weight * light_ref[side, rank, rows_of(i)]
                        clear = left
                        sums = [
                            acc + weight * grow(cubic(table[j], value), True)
                            for j, acc in enumerate(sums)
                        ]
                    return clear, sums

                zero = jnp.zeros(shape, jnp.float32)
                clear, sums = lax.fori_loop(
                    0, steps, step, (jnp.ones(shape, jnp.float32), [zero, zero, zero])
                )
                finish(m, plane, clear, sums)

        return carry

    @pl.when(jnp.logical_not(jnp.min(margins[0]) > 0.0))
    def _():
        lax.fori_loop(0, images, image, 0)


def render(cells, picked, coeffs, index, fields, *edges):
    images = index.shape[0]
    planes = fields.shape[0]
    vmem = pl.BlockSpec(memory_space=pltpu.VMEM)
    smem = pl.BlockSpec(memory_space=pltpu.SMEM)
    points = images * len(picked) * cells * LANES
    poly = (images * 4 * 2 * SEGS, len(picked) * LANES)
    table = (poly[0], TERMS * 2 * SEGS)
    picture = jax.ShapeDtypeStruct((images, 4, planes, LANES), jnp.float32)
    any_space = pl.BlockSpec(memory_space=pl.ANY)
    first = not edges
    return pl.pallas_call(
        functools.partial(render_kernel, cells, picked),
        in_specs=[smem, smem, any_space] + ([] if first else [vmem, any_space, vmem, vmem]),
        out_specs=[vmem, vmem] if first else vmem,
        out_shape=[picture, jax.ShapeDtypeStruct(table, jnp.bfloat16)] if first else picture,
        scratch_shapes=([] if first else [pltpu.VMEM((2, *fields.shape[1:]), jnp.float32)])
        + [
            pltpu.VMEM(fields.shape, jnp.float32),
            pltpu.VMEM((len(picked), *fields.shape[1:]), jnp.float32),
            pltpu.VMEM(table, jnp.bfloat16),
            pltpu.VMEM((images, len(picked), 4, SEGS, LANES), jnp.float32),
            pltpu.SemaphoreType.DMA((2,)),
        ]
        + [pltpu.VMEM(poly, jnp.float32)] * 4,
        cost_estimate=pl.CostEstimate(
            flops=64 * points, bytes_accessed=4 * 2**20, transcendentals=9 * points
        ),
        name="render",
        compiler_params=pltpu.CompilerParams(vmem_limit_bytes=RENDER_LIMIT),
    )(coeffs, index, fields, *edges)


def shifts(axis):
    devices = lax.axis_size(axis)
    up = [(i, (i + 1) % devices) for i in range(devices)]
    return up, [(j, i) for i, j in up]


def fast_body(spectrum, transfer_coeffs, transfer_index):
    _, rows, planes, nx = spectrum.shape
    blocks = lax.axis_size("depth")
    nz = rows * blocks
    x_table = x_tables(nx, blocks)
    zhi, zlo, twiddle = z_tables(nz)
    me = lax.axis_index("depth")[None]
    modes = spectrum.reshape(2 * rows * planes, blocks, LANES).transpose(1, 0, 2)
    sent = [None] * blocks
    for pair in PAIRS:
        made = x_transform(modes, me, pair, planes, x_table)
        for step, block in zip(pair, made):
            swap = [(i, i ^ step) for i in range(blocks)]
            sent[step] = lax.ppermute(block, "depth", swap) if step else block
    fields, low, high, slabs = z_transform(me, sent, planes, zhi, zlo, twiddle)
    up, down = shifts("plane")
    before = lax.ppermute(high, "plane", up)
    after = lax.ppermute(low, "plane", down)
    slabs = lax.all_to_all(
        slabs.reshape(blocks, rows, planes, LANES), "depth", split_axis=0, concat_axis=0, tiled=True
    )
    scalar_field = slabs.transpose(1, 2, 0, 3).reshape(rows, planes, nx)
    inner = tuple(range(1, planes - 1))
    picture, table = render(nz, inner, transfer_coeffs, transfer_index, fields)
    rendered = render(
        nz, (0, planes - 1), transfer_coeffs, transfer_index, fields, picture, table, before, after
    )
    return scalar_field, rendered


def with_halo(array, sides, width):
    for axis, dim in sides:
        devices, length = (lax.axis_size(axis), array.shape[dim])
        up = [(i, (i + 1) % devices) for i in range(devices)]
        down = [(j, i) for i, j in up]
        last = lax.slice_in_dim(array, length - width, length, axis=dim)
        first = lax.slice_in_dim(array, 0, width, axis=dim)
        before = lax.ppermute(last, axis, up)
        after = lax.ppermute(first, axis, down)
        array = jnp.concatenate([before, array, after], axis=dim)
    return array


def dft_tables(length):
    indices = jnp.arange(length, dtype=jnp.int32)
    phase_index = indices[:, None] * indices[None, :] % length
    angles = phase_index.astype(jnp.float32) * (2.0 * jnp.pi / length)
    scaling = 1.0 / jnp.sqrt(jnp.float32(length))
    return (jnp.cos(angles) * scaling, jnp.sin(angles) * scaling)


def polynomial(coeffs, values):
    result = coeffs[-1] + jnp.zeros_like(values)
    for degree in range(coeffs.shape[0] - 2, -1, -1):
        result = result * values + coeffs[degree]
    return result


def plane_slope(field_cells):
    padded = with_halo(field_cells, (("plane", 1),), 1)
    return 0.5 * (padded[:, 2:] - padded[:, :-2])


def render_blocks(field_cells, slope_cells, selected, blocks):
    depth_cells, plane_count, column_count = field_cells.shape
    block_cells = depth_cells // blocks
    values = field_cells.reshape(blocks, block_cells, plane_count, column_count)
    lighting = 1.0 + shade_gain * jnp.tanh(
        slope_cells.reshape(blocks, block_cells, plane_count, column_count)
    )
    per_image = []
    for which_image in range(selected.shape[0]):
        coeffs = selected[which_image]
        optical = jax.nn.softplus(polynomial(coeffs[3], values)) * (density / depth_cells)
        before = jnp.cumsum(optical, axis=1) - optical
        weight = jnp.exp(-before) * -jnp.expm1(-optical) * lighting
        block_depth = jnp.sum(optical, axis=1)
        ahead = jnp.cumsum(block_depth, axis=0) - block_depth
        reach = jnp.exp(-ahead)
        channels = []
        for channel in range(3):
            glow_cells = jax.nn.softplus(polynomial(coeffs[channel], values))
            channels.append(jnp.sum(reach * jnp.sum(weight * glow_cells, axis=1), axis=0))
        channels.append(jnp.sum(block_depth, axis=0))
        per_image.append(jnp.stack(channels))
    return jnp.stack(per_image)


def body(spectrum, transfer_coeffs, transfer_index):
    _, rows, _, nx = spectrum.shape
    cos_z, sin_z = dft_tables(rows * lax.axis_size("depth"))
    cos_x, sin_x = dft_tables(nx)
    one_hot = (
        transfer_index[:, None] == jnp.arange(transfer_coeffs.shape[0], dtype=jnp.int32)[None, :]
    ).astype(jnp.float32)
    selected = jnp.sum(one_hot[:, :, None, None] * transfer_coeffs[None], axis=1)
    depth_count = lax.axis_size("depth")
    real_part = spectrum[0].astype(jnp.float32)
    imag_part = spectrum[1].astype(jnp.float32)
    h_re = jnp.einsum("zpk,kx->zpx", real_part, cos_x, precision=highest) - jnp.einsum(
        "zpk,kx->zpx", imag_part, sin_x, precision=highest
    )
    h_im = jnp.einsum("zpk,kx->zpx", real_part, sin_x, precision=highest) + jnp.einsum(
        "zpk,kx->zpx", imag_part, cos_x, precision=highest
    )
    mixed = jnp.stack([h_re, h_im])
    arrived = lax.all_to_all(mixed, "depth", split_axis=3, concat_axis=1, tiled=True)
    field_columns = jnp.einsum("zk,kpx->zpx", cos_z, arrived[0], precision=highest) - jnp.einsum(
        "zk,kpx->zpx", sin_z, arrived[1], precision=highest
    )
    slope_cells = plane_slope(field_columns)
    merged = render_blocks(field_columns, slope_cells, selected, depth_count)
    scalar_field = lax.all_to_all(field_columns, "depth", split_axis=0, concat_axis=2, tiled=True)
    rendered = jnp.concatenate([merged[:, :3], jnp.exp(-merged[:, 3:4])], axis=1)
    return (scalar_field, rendered)


def solution(mesh):
    def pick(spectrum, *rest):
        _, rows, planes, nx = spectrum.shape
        blocks = lax.axis_size("depth")
        if nx == LANES * blocks and blocks == SEGS and planes == 4 and rows % PACK == 0:
            return fast_body(spectrum, *rest)
        return body(spectrum, *rest)

    return jax.shard_map(
        pick,
        mesh=mesh,
        in_specs=(P(None, "depth", "plane", None), P(), P()),
        out_specs=(P("depth", "plane", None), P(None, None, "plane", "depth")),
        check_vma=False,
    )
```

```python
import functools

import jax
import jax.numpy as jnp
import numpy as np
from jax import lax
from jax.experimental import pallas as pl
from jax.experimental.pallas import tpu as pltpu
from jax.sharding import PartitionSpec as P


density = 2.0
shade_gain = 0.4
highest = lax.Precision.HIGHEST
LANES = 128
SEGS = 8
RADIX = 4
PACK = 16
PAIRS = ((6, 7), (2, 3), (4, 5), (1, 0))
LEVELS = 16.0
STEPS = 32766.0
TINY = 2.0**-108
FAINT = 2.0**-9
SPARSE = 0.02
TERMS = 16
VMEM_LIMIT = 14 * 2**20
RENDER_LIMIT = 14 * 2**20
LOG2E = 1.4426950408889634
LN2 = 0.6931471805599453


def split_table(table):
    hi = table.astype(jnp.bfloat16)
    lo = (table - hi.astype(np.float64)).astype(jnp.bfloat16)
    return hi, lo


def x_tables(nx, blocks):
    k = np.arange(nx, dtype=np.int64)
    angle = 2.0 * np.pi * ((k[:, None] * k[None, :]) % nx) / nx
    cols = nx // blocks
    cos = (np.cos(angle) / np.sqrt(nx)).reshape(nx, blocks, cols)
    sin = (np.sin(angle) / np.sqrt(nx)).reshape(nx, blocks, cols)
    hi, lo = split_table(np.concatenate([cos, sin], axis=2).transpose(1, 0, 2))
    return jnp.asarray(np.concatenate([hi, lo], axis=2)[: blocks // RADIX])


def z_tables(nz):
    quarter = nz // RADIX
    q = np.arange(quarter, dtype=np.int64)
    steps = quarter // SEGS
    row = np.arange(quarter)
    m = (row % SEGS) * steps + row // SEGS
    angle = 2.0 * np.pi * ((m[:, None] * q[None, :]) % quarter) / quarter
    table = np.concatenate([np.cos(angle), -np.sin(angle)], axis=1) / np.sqrt(nz)
    turn = 2.0 * np.pi * np.arange(1, RADIX)[:, None] * q[None, :] / nz
    twiddle = np.stack([np.cos(turn), np.sin(turn)], axis=1)
    wide = np.broadcast_to(twiddle[..., None], twiddle.shape + (LANES,))
    hi, lo = split_table(table)
    return jnp.asarray(hi), jnp.asarray(lo), jnp.asarray(wide, jnp.float32)


def level_of(peak):
    level = jnp.ceil(LEVELS * jnp.log2(jnp.maximum(peak, TINY))) + 1.0
    return level, STEPS * jnp.exp2(level * (-1.0 / LEVELS))


def code(value, scale):
    return jnp.round(value * scale).astype(jnp.int32).astype(jnp.int16)


def decode(whole, scale):
    return whole.astype(jnp.int32).astype(jnp.float32) * scale


def step_of(level):
    return jnp.exp2(level * (1.0 / LEVELS)) * (1.0 / STEPS)


def x_kernel(planes, blocks, pair, target_ref, spec_ref, table_ref, *refs):
    outs, (mixed_ref,) = refs[:-1], refs[-1:]
    half = spec_ref.shape[1] // 2
    rows = half // planes
    cols = table_ref.shape[2] // 4
    step = jnp.where(pl.program_id(0) == 0, pair[0], pair[1])
    turns = jnp.bitwise_xor(target_ref[0], step) // (blocks // RADIX)
    row = lax.broadcasted_iota(jnp.int32, (PACK, cols), 0)
    phase = (row % RADIX * turns) % RADIX
    cosine = jnp.where(phase == 0, 1.0, jnp.where(phase == 2, -1.0, 0.0)).astype(jnp.bfloat16)
    sine = jnp.where(phase == 1, 1.0, jnp.where(phase == 3, -1.0, 0.0)).astype(jnp.bfloat16)

    def turned(at):
        parts = [
            table_ref[0, at : at + PACK, part * cols : (part + 1) * cols] for part in range(4)
        ]
        made = []
        for c, s in (parts[:2], parts[2:]):
            made += [c * cosine - s * sine, c * sine + s * cosine]
        return jnp.concatenate(made, axis=1)

    table = jnp.concatenate([turned(at) for at in range(0, table_ref.shape[1], PACK)], axis=0)

    def product(part):
        own = slice(part * half, (part + 1) * half)
        modes = jnp.concatenate([spec_ref[at, own] for at in range(spec_ref.shape[0])], axis=1)
        both = jnp.dot(modes, table, preferred_element_type=jnp.float32)
        return both[:, : 2 * cols] + both[:, 2 * cols :]

    a = product(0)
    b = product(1)
    mixed_ref[0] = a[:, :cols] - b[:, cols:]
    mixed_ref[1] = a[:, cols:] + b[:, :cols]
    place = lax.broadcasted_iota(jnp.int32, (PACK, cols), 0)

    def emit(out_ref):
        levels = jnp.zeros((PACK, cols), jnp.float32)
        for plane in range(planes):
            parts = [mixed_ref[part, pl.ds(plane, rows, stride=planes)] for part in range(2)]
            peak = jnp.maximum(jnp.abs(parts[0]), jnp.abs(parts[1]))
            peak = jnp.max(peak, axis=0, keepdims=True)
            level, scale = level_of(peak)
            for part in range(2):
                at = (plane * 2 + part) * rows
                out_ref[at : at + rows] = code(parts[part], scale)
            levels = jnp.where(place == plane, jnp.broadcast_to(level, levels.shape), levels)
        at = planes * 2 * rows
        out_ref[at : at + PACK] = levels.astype(jnp.int32).astype(jnp.int16)

    for which, out_ref in enumerate(outs):
        pl.when(pl.program_id(0) == which)(functools.partial(emit, out_ref))


def x_transform(spec, me, pair, planes, tables):
    tiles, modes, lanes = spec.shape
    nx = tiles * lanes
    _, _, wide = tables.shape
    cols = wide // 4
    count = len(pair)
    sent = (modes + PACK, cols)

    def table(d, t):
        return (jnp.bitwise_xor(t[0], jnp.where(d == 0, pair[0], pair[1])) % (tiles // RADIX), 0, 0)

    return pl.pallas_call(
        functools.partial(x_kernel, planes, tiles, pair),
        grid_spec=pltpu.PrefetchScalarGridSpec(
            num_scalar_prefetch=1,
            grid=(count,),
            in_specs=[
                pl.BlockSpec(memory_space=pltpu.VMEM),
                pl.BlockSpec((1, nx, wide), table),
            ],
            out_specs=[pl.BlockSpec(sent, lambda d, t: (0, 0))] * count,
            scratch_shapes=[pltpu.VMEM((2, modes // 2, cols), jnp.float32)],
        ),
        out_shape=[jax.ShapeDtypeStruct(sent, jnp.int16)] * count,
        cost_estimate=pl.CostEstimate(
            flops=2 * modes * nx * wide * count,
            bytes_accessed=2 * modes * nx + 2 * nx * wide * count,
            transcendentals=0,
        ),
        name="x_transform",
        compiler_params=pltpu.CompilerParams(vmem_limit_bytes=VMEM_LIMIT),
    )(me, spec, tables)


def z_kernel(me_ref, *refs):
    blocks = SEGS
    sent, refs = refs[:blocks], refs[blocks:]
    hi_ref, lo_ref, twiddle_ref, out_ref, low_ref, high_ref, slab_ref = refs[:7]
    in_ref, yhi_ref, ylo_ref, sem = refs[7:]
    plane = pl.program_id(0)
    planes = pl.num_programs(0)
    _, total, cols = in_ref.shape
    quarter = hi_ref.shape[0]
    rows = quarter * RADIX // blocks
    per = blocks // RADIX

    @pl.when(plane == 0)
    def _():
        copies = [
            pltpu.make_async_copy(ref, in_ref.at[jnp.bitwise_xor(me_ref[0], step)], sem.at[step])
            for step, ref in enumerate(sent)
        ]
        for copy in copies:
            copy.start()
        for copy in copies:
            copy.wait()

    def split(value, row, rank):
        high = value.astype(jnp.bfloat16)
        yhi_ref[pl.ds(row, PACK), rank * cols : (rank + 1) * cols] = high
        ylo_ref[pl.ds(row, PACK), rank * cols : (rank + 1) * cols] = (
            value - high.astype(jnp.float32)
        ).astype(jnp.bfloat16)

    place = lax.broadcasted_iota(jnp.int32, (PACK, cols), 0)

    def scale_of(source):
        level = in_ref[source, total - PACK : total].astype(jnp.int32).astype(jnp.float32)
        level = jnp.sum(jnp.where(place == plane, level, 0.0), axis=0, keepdims=True)
        return step_of(level)

    base = pl.multiple_of(plane * (2 * rows), 2 * rows)
    for block in range(per):
        sources = [t * per + block for t in range(RADIX)]
        scales = [jnp.broadcast_to(scale_of(source), (PACK, cols)) for source in sources]

        def load(t, part, chunk):
            start = pl.multiple_of(base + part * rows + chunk, PACK)
            return decode(in_ref[sources[t], pl.ds(start, PACK)], scales[t])

        def turn(nth, carry):
            chunk = nth * PACK
            re = [load(t, 0, chunk) for t in range(RADIX)]
            im = [load(t, 1, chunk) for t in range(RADIX)]
            row = pl.multiple_of(block * rows + chunk, PACK)
            even_re, even_im = re[0] + re[2], im[0] + im[2]
            diff_re, diff_im = re[0] - re[2], im[0] - im[2]
            odd_re, odd_im = re[1] + re[3], im[1] + im[3]
            side_re, side_im = re[1] - re[3], im[1] - im[3]
            sums = (
                (even_re + odd_re, even_im + odd_im),
                (diff_re - side_im, diff_im + side_re),
                (even_re - odd_re, even_im - odd_im),
                (diff_re + side_im, diff_im - side_re),
            )
            for rank in range(RADIX):
                a, b = sums[rank]
                if rank > 0:
                    c = twiddle_ref[rank - 1, 0, pl.ds(row, PACK)]
                    s = twiddle_ref[rank - 1, 1, pl.ds(row, PACK)]
                    a, b = a * c - b * s, a * s + b * c
                split(a, row, rank)
                split(b, quarter + row, rank)
            return carry

        lax.fori_loop(0, rows // PACK, turn, 0, unroll=2)
    for pair in range(0, RADIX, 2):
        at = slice(pair * cols, (pair + 2) * cols)
        high = yhi_ref[:, at]
        value = (
            jnp.dot(hi_ref[...], high, preferred_element_type=jnp.float32)
            + jnp.dot(hi_ref[...], ylo_ref[:, at], preferred_element_type=jnp.float32)
            + jnp.dot(lo_ref[...], high, preferred_element_type=jnp.float32)
        )
        out_ref[0, pair] = value[:, :cols]
        out_ref[0, pair + 1] = value[:, cols:]

    def edge(edge_ref):
        peak = jnp.max(jnp.abs(out_ref[0, 0]), axis=0, keepdims=True)
        for rank in range(1, RADIX):
            peak = jnp.maximum(peak, jnp.max(jnp.abs(out_ref[0, rank]), axis=0, keepdims=True))
        level, scale = level_of(peak)
        for rank in range(RADIX):
            edge_ref[rank * quarter : (rank + 1) * quarter] = code(out_ref[0, rank], scale)
        level = jnp.broadcast_to(level, (PACK, cols)).astype(jnp.int32)
        edge_ref[RADIX * quarter :] = level.astype(jnp.int16)

    pl.when(plane == 0)(functools.partial(edge, low_ref))
    pl.when(plane == planes - 1)(functools.partial(edge, high_ref))

    steps = quarter // SEGS
    count = slab_ref.shape[1] // (RADIX * steps)
    for seg in range(SEGS):
        for rank in range(RADIX):
            values = out_ref[0, rank, pl.ds(seg, steps, stride=SEGS)]
            slab_ref[seg, pl.ds(rank * count + plane, steps, stride=RADIX * count)] = values


def z_transform(me, sent, planes, hi, lo, twiddle):
    total, cols = sent[0].shape
    blocks = len(sent)
    quarter = hi.shape[0]
    field = (RADIX, quarter, cols)
    edge = (RADIX * quarter + PACK, cols)
    slabs = (SEGS, RADIX * quarter // SEGS * planes, cols)
    return pl.pallas_call(
        z_kernel,
        grid=(planes,),
        in_specs=[pl.BlockSpec(memory_space=pltpu.SMEM)]
        + [pl.BlockSpec(memory_space=pl.ANY)] * blocks
        + [
            pl.BlockSpec(hi.shape, lambda p: (0, 0)),
            pl.BlockSpec(lo.shape, lambda p: (0, 0)),
            pl.BlockSpec(twiddle.shape, lambda p: (0, 0, 0, 0)),
        ],
        out_specs=[
            pl.BlockSpec((1, *field), lambda p: (p, 0, 0, 0)),
            pl.BlockSpec(edge, lambda p: (0, 0)),
            pl.BlockSpec(edge, lambda p: (0, 0)),
            pl.BlockSpec(slabs, lambda p: (0, 0, 0)),
        ],
        out_shape=[
            jax.ShapeDtypeStruct((planes, *field), jnp.float32),
            jax.ShapeDtypeStruct(edge, jnp.int16),
            jax.ShapeDtypeStruct(edge, jnp.int16),
            jax.ShapeDtypeStruct(slabs, jnp.float32),
        ],
        scratch_shapes=[
            pltpu.VMEM((blocks, total, cols), jnp.int16),
            pltpu.VMEM((2 * quarter, RADIX * cols), jnp.bfloat16),
            pltpu.VMEM((2 * quarter, RADIX * cols), jnp.bfloat16),
            pltpu.SemaphoreType.DMA((blocks,)),
        ],
        cost_estimate=pl.CostEstimate(
            flops=2 * planes * quarter * 2 * quarter * RADIX * cols * 3,
            bytes_accessed=6 * 2**20,
            transcendentals=0,
        ),
        name="z_transform",
        compiler_params=pltpu.CompilerParams(vmem_limit_bytes=VMEM_LIMIT),
    )(me, *sent, hi, lo, twiddle)


def grow(power, careful):
    grown = jnp.exp2(jnp.minimum(power, 126.0))
    soft = jnp.log2(1.0 + grown)
    if careful:
        soft = jnp.where(grown < 2.0**-12, grown * LOG2E, soft)
    return jnp.maximum(soft, power)


def cubic(coeffs, value):
    return ((coeffs[3] * value + coeffs[2]) * value + coeffs[1]) * value + coeffs[0]


def halves(value):
    high = value.astype(jnp.bfloat16).astype(jnp.float32)
    return high, (value - high).astype(jnp.bfloat16).astype(jnp.float32)


def render_kernel(cells, picked, coeffs_ref, index_ref, field_ref, *refs):
    first = len(refs) == 10
    if first:
        out_ref, table_ref, *refs = refs
    else:
        done_ref, table_ref, *halo_refs, out_ref, edge_ref = refs[:6]
        refs = refs[6:]
        before_ref, after_ref = edge_ref.at[0], edge_ref.at[1]
        out_ref[...] = done_ref[...]
    light_ref, lhs_ref, state_ref, sem, *refs = refs
    banks = (refs[0:2], refs[2:4])
    loads = [] if first else [pltpu.make_async_copy(table_ref, lhs_ref, sem.at[0])]
    for load in loads:
        load.start()
    steps = field_ref.shape[2] // SEGS
    images = index_ref.shape[0]
    last = field_ref.shape[0] - 1
    shape = (SEGS, LANES)
    tall = 2 * SEGS
    wide = len(picked) * LANES

    def rows_of(i):
        return pl.ds(pl.multiple_of(i * SEGS, SEGS), SEGS)

    def coeffs_of(m, j):
        return [coeffs_ref[index_ref[m], j, n] * LOG2E for n in range(4)]

    lane = lax.broadcasted_iota(jnp.int32, (tall, TERMS * tall), 1)
    row = lax.broadcasted_iota(jnp.int32, (tall, TERMS * tall), 0)
    term = jnp.where(lane % tall == row, lane // tall, -1)

    def lay(m, carry):
        for j in range(4):
            splits = [halves(jnp.full((1, LANES), c, jnp.float32)) for c in coeffs_of(m, j)]
            full = jnp.full((1, LANES), coeffs_of(m, j)[0], jnp.float32)
            weights = [*splits[0], full - splits[0][0] - splits[0][1]]
            for n in range(1, 4):
                weights += [*splits[n], *splits[n]]
            tile = jnp.zeros((tall, TERMS * tall), jnp.float32)
            for at, weight in enumerate(weights):
                spread = jnp.broadcast_to(weight[:, :1], tile.shape)
                tile = jnp.where(term == at, spread, tile)
            start = pl.multiple_of((m * 4 + j) * tall, tall)
            lhs_ref[pl.ds(start, tall)] = tile.astype(jnp.bfloat16)
        return carry

    if first:
        lax.fori_loop(0, images, lay, 0)
        table_ref[...] = lhs_ref[...]
    else:
        for nth, halo_ref in enumerate(halo_refs):
            level = halo_ref[RADIX * steps * SEGS :].astype(jnp.int32).astype(jnp.float32)
            scale = step_of(level[0:1])
            for rank in range(RADIX):
                rows = slice(rank * steps * SEGS, (rank + 1) * steps * SEGS)
                edge_ref[nth, rank] = decode(halo_ref[rows], scale)
    for load in loads:
        load.wait()
    for side, plane in enumerate(picked):
        below = before_ref if plane == 0 else field_ref.at[plane - 1]
        above = after_ref if plane == last else field_ref.at[plane + 1]

        def light(i, carry):
            for rank in range(RADIX):
                slope = 0.5 * (above[rank, rows_of(i)] - below[rank, rows_of(i)])
                light_ref[side, rank, rows_of(i)] = 1.0 + shade_gain * jnp.tanh(slope)
            return carry

        lax.fori_loop(0, steps, light, 0, unroll=2)

    one = jnp.ones((tall, wide), jnp.bfloat16)

    def powers(i, bank):
        for half, poly_ref in enumerate(bank):
            value = jnp.concatenate(
                [
                    jnp.concatenate(
                        [field_ref[plane, 2 * half + odd, rows_of(i)] for plane in picked], axis=1
                    )
                    for odd in range(2)
                ],
                axis=0,
            )
            terms = [one, one, one]
            power = value
            for _ in range(3):
                high = power.astype(jnp.bfloat16)
                low = (power - high.astype(jnp.float32)).astype(jnp.bfloat16)
                terms += [high, high, low, low]
                power = power * value
            terms += [one] * (TERMS - len(terms))
            poly_ref[...] = jnp.dot(
                lhs_ref[...], jnp.concatenate(terms, axis=0), preferred_element_type=jnp.float32
            )

    def absorb(i, bank):
        for m in range(images):
            for side in range(len(picked)):
                clear = state_ref[m, side, 3]
                sums = [state_ref[m, side, j] for j in range(3)]
                for rank in range(RADIX):
                    poly_ref = bank[rank // 2]

                    def poly(j):
                        at = (m * 4 + j) * tall + (rank % 2) * SEGS
                        return poly_ref[at : at + SEGS, side * LANES : (side + 1) * LANES]

                    left = clear * jnp.exp2(grow(poly(3), False) * (-density / cells))
                    weight = (clear - left) * light_ref[side, rank, rows_of(i)]
                    clear = left
                    sums = [acc + weight * grow(poly(j), False) for j, acc in enumerate(sums)]
                state_ref[m, side, 3] = clear
                for j in range(3):
                    state_ref[m, side, j] = sums[j]

    state_ref[:, :, 0:3] = jnp.zeros((images, len(picked), 3, *shape), jnp.float32)
    state_ref[:, :, 3] = jnp.ones((images, len(picked), *shape), jnp.float32)
    powers(0, banks[0])
    powers(1, banks[1])

    def pair(k, carry):
        absorb(2 * k, banks[0])
        absorb(2 * k + 1, banks[1])
        powers(jnp.minimum(2 * k + 2, steps - 2), banks[0])
        powers(jnp.minimum(2 * k + 3, steps - 1), banks[1])
        return carry

    lax.fori_loop(0, steps // 2, pair, 0)

    seg = lax.broadcasted_iota(jnp.int32, shape, 0)

    def finish(m, plane, clear, sums):
        reach = jnp.where(seg == 0, 1.0, pltpu.roll(clear, 1, 0))
        for shift in (1, 2, 4):
            reach = reach * jnp.where(seg < shift, 1.0, pltpu.roll(reach, shift, 0))
        totals = [jnp.sum(reach * acc, axis=0, keepdims=True) for acc in sums]
        clear = (reach * clear)[SEGS - 1 :]
        for j in range(3):
            out_ref[m, j, plane : plane + 1] = totals[j] * LN2
        out_ref[m, 3, plane : plane + 1] = clear
        least = jnp.minimum(jnp.minimum(totals[0], totals[1]), totals[2])
        taken = 1.0 - clear
        return jnp.minimum(least - FAINT * taken, taken - SPARSE)

    margins = []
    for m in range(images):
        for side, plane in enumerate(picked):
            sums = [state_ref[m, side, j] for j in range(3)]
            margins.append(finish(m, plane, state_ref[m, side, 3], sums))
    while len(margins) > 1:
        margins = [
            jnp.minimum(a, b) for a, b in zip(margins[::2], margins[1::2])
        ]

    def image(m, carry):
        for side, plane in enumerate(picked):
            sums = [state_ref[m, side, j] for j in range(3)]
            margin = jnp.min(finish(m, plane, state_ref[m, side, 3], sums))

            @pl.when(jnp.logical_not(margin > 0.0))
            def _():
                table = [
                    [jnp.full(shape, c, jnp.float32) for c in coeffs_of(m, j)] for j in range(4)
                ]

                def step(i, state):
                    clear, sums = state
                    for rank in range(RADIX):
                        value = field_ref[plane, rank, rows_of(i)]
                        depth = grow(cubic(table[3], value), True) * (-density / cells)
                        left = clear * jnp.exp2(depth)
                        near = clear * depth * (-LN2 - (0.5 * LN2 * LN2) * depth)
                        weight = jnp.where(depth > -(2.0**-9), near, clear - left)
                        weight = weight * light_ref[side, rank, rows_of(i)]
                        clear = left
                        sums = [
                            acc + weight * grow(cubic(table[j], value), True)
                            for j, acc in enumerate(sums)
                        ]
                    return clear, sums

                zero = jnp.zeros(shape, jnp.float32)
                clear, sums = lax.fori_loop(
                    0, steps, step, (jnp.ones(shape, jnp.float32), [zero, zero, zero])
                )
                finish(m, plane, clear, sums)

        return carry

    @pl.when(jnp.logical_not(jnp.min(margins[0]) > 0.0))
    def _():
        lax.fori_loop(0, images, image, 0)


def render(cells, picked, coeffs, index, fields, *edges):
    images = index.shape[0]
    planes = fields.shape[0]
    vmem = pl.BlockSpec(memory_space=pltpu.VMEM)
    smem = pl.BlockSpec(memory_space=pltpu.SMEM)
    points = images * len(picked) * cells * LANES
    poly = (images * 4 * 2 * SEGS, len(picked) * LANES)
    table = (poly[0], TERMS * 2 * SEGS)
    picture = jax.ShapeDtypeStruct((images, 4, planes, LANES), jnp.float32)
    any_space = pl.BlockSpec(memory_space=pl.ANY)
    first = not edges
    return pl.pallas_call(
        functools.partial(render_kernel, cells, picked),
        in_specs=[smem, smem, vmem] + ([] if first else [vmem, any_space, vmem, vmem]),
        out_specs=[vmem, vmem] if first else vmem,
        out_shape=[picture, jax.ShapeDtypeStruct(table, jnp.bfloat16)] if first else picture,
        scratch_shapes=([] if first else [pltpu.VMEM((2, *fields.shape[1:]), jnp.float32)])
        + [
            pltpu.VMEM((len(picked), *fields.shape[1:]), jnp.float32),
            pltpu.VMEM(table, jnp.bfloat16),
            pltpu.VMEM((images, len(picked), 4, SEGS, LANES), jnp.float32),
            pltpu.SemaphoreType.DMA((1,)),
        ]
        + [pltpu.VMEM(poly, jnp.float32)] * 4,
        cost_estimate=pl.CostEstimate(
            flops=64 * points, bytes_accessed=4 * 2**20, transcendentals=9 * points
        ),
        name="render",
        compiler_params=pltpu.CompilerParams(vmem_limit_bytes=RENDER_LIMIT),
    )(coeffs, index, fields, *edges)


def shifts(axis):
    devices = lax.axis_size(axis)
    up = [(i, (i + 1) % devices) for i in range(devices)]
    return up, [(j, i) for i, j in up]


def fast_body(spectrum, transfer_coeffs, transfer_index):
    _, rows, planes, nx = spectrum.shape
    blocks = lax.axis_size("depth")
    nz = rows * blocks
    x_table = x_tables(nx, blocks)
    zhi, zlo, twiddle = z_tables(nz)
    me = lax.axis_index("depth")[None]
    modes = spectrum.reshape(2 * rows * planes, blocks, LANES).transpose(1, 0, 2)
    sent = [None] * blocks
    for pair in PAIRS:
        made = x_transform(modes, me, pair, planes, x_table)
        for step, block in zip(pair, made):
            swap = [(i, i ^ step) for i in range(blocks)]
            sent[step] = lax.ppermute(block, "depth", swap) if step else block
    fields, low, high, slabs = z_transform(me, sent, planes, zhi, zlo, twiddle)
    up, down = shifts("plane")
    before = lax.ppermute(high, "plane", up)
    after = lax.ppermute(low, "plane", down)
    slabs = lax.all_to_all(
        slabs.reshape(blocks, rows, planes, LANES), "depth", split_axis=0, concat_axis=0, tiled=True
    )
    scalar_field = slabs.transpose(1, 2, 0, 3).reshape(rows, planes, nx)
    inner = tuple(range(1, planes - 1))
    picture, table = render(nz, inner, transfer_coeffs, transfer_index, fields)
    rendered = render(
        nz, (0, planes - 1), transfer_coeffs, transfer_index, fields, picture, table, before, after
    )
    return scalar_field, rendered


def with_halo(array, sides, width):
    for axis, dim in sides:
        devices, length = (lax.axis_size(axis), array.shape[dim])
        up = [(i, (i + 1) % devices) for i in range(devices)]
        down = [(j, i) for i, j in up]
        last = lax.slice_in_dim(array, length - width, length, axis=dim)
        first = lax.slice_in_dim(array, 0, width, axis=dim)
        before = lax.ppermute(last, axis, up)
        after = lax.ppermute(first, axis, down)
        array = jnp.concatenate([before, array, after], axis=dim)
    return array


def dft_tables(length):
    indices = jnp.arange(length, dtype=jnp.int32)
    phase_index = indices[:, None] * indices[None, :] % length
    angles = phase_index.astype(jnp.float32) * (2.0 * jnp.pi / length)
    scaling = 1.0 / jnp.sqrt(jnp.float32(length))
    return (jnp.cos(angles) * scaling, jnp.sin(angles) * scaling)


def polynomial(coeffs, values):
    result = coeffs[-1] + jnp.zeros_like(values)
    for degree in range(coeffs.shape[0] - 2, -1, -1):
        result = result * values + coeffs[degree]
    return result


def plane_slope(field_cells):
    padded = with_halo(field_cells, (("plane", 1),), 1)
    return 0.5 * (padded[:, 2:] - padded[:, :-2])


def render_blocks(field_cells, slope_cells, selected, blocks):
    depth_cells, plane_count, column_count = field_cells.shape
    block_cells = depth_cells // blocks
    values = field_cells.reshape(blocks, block_cells, plane_count, column_count)
    lighting = 1.0 + shade_gain * jnp.tanh(
        slope_cells.reshape(blocks, block_cells, plane_count, column_count)
    )
    per_image = []
    for which_image in range(selected.shape[0]):
        coeffs = selected[which_image]
        optical = jax.nn.softplus(polynomial(coeffs[3], values)) * (density / depth_cells)
        before = jnp.cumsum(optical, axis=1) - optical
        weight = jnp.exp(-before) * -jnp.expm1(-optical) * lighting
        block_depth = jnp.sum(optical, axis=1)
        ahead = jnp.cumsum(block_depth, axis=0) - block_depth
        reach = jnp.exp(-ahead)
        channels = []
        for channel in range(3):
            glow_cells = jax.nn.softplus(polynomial(coeffs[channel], values))
            channels.append(jnp.sum(reach * jnp.sum(weight * glow_cells, axis=1), axis=0))
        channels.append(jnp.sum(block_depth, axis=0))
        per_image.append(jnp.stack(channels))
    return jnp.stack(per_image)


def body(spectrum, transfer_coeffs, transfer_index):
    _, rows, _, nx = spectrum.shape
    cos_z, sin_z = dft_tables(rows * lax.axis_size("depth"))
    cos_x, sin_x = dft_tables(nx)
    one_hot = (
        transfer_index[:, None] == jnp.arange(transfer_coeffs.shape[0], dtype=jnp.int32)[None, :]
    ).astype(jnp.float32)
    selected = jnp.sum(one_hot[:, :, None, None] * transfer_coeffs[None], axis=1)
    depth_count = lax.axis_size("depth")
    real_part = spectrum[0].astype(jnp.float32)
    imag_part = spectrum[1].astype(jnp.float32)
    h_re = jnp.einsum("zpk,kx->zpx", real_part, cos_x, precision=highest) - jnp.einsum(
        "zpk,kx->zpx", imag_part, sin_x, precision=highest
    )
    h_im = jnp.einsum("zpk,kx->zpx", real_part, sin_x, precision=highest) + jnp.einsum(
        "zpk,kx->zpx", imag_part, cos_x, precision=highest
    )
    mixed = jnp.stack([h_re, h_im])
    arrived = lax.all_to_all(mixed, "depth", split_axis=3, concat_axis=1, tiled=True)
    field_columns = jnp.einsum("zk,kpx->zpx", cos_z, arrived[0], precision=highest) - jnp.einsum(
        "zk,kpx->zpx", sin_z, arrived[1], precision=highest
    )
    slope_cells = plane_slope(field_columns)
    merged = render_blocks(field_columns, slope_cells, selected, depth_count)
    scalar_field = lax.all_to_all(field_columns, "depth", split_axis=0, concat_axis=2, tiled=True)
    rendered = jnp.concatenate([merged[:, :3], jnp.exp(-merged[:, 3:4])], axis=1)
    return (scalar_field, rendered)


def solution(mesh):
    def pick(spectrum, *rest):
        _, rows, planes, nx = spectrum.shape
        blocks = lax.axis_size("depth")
        if nx == LANES * blocks and blocks == SEGS and planes == 4 and rows % PACK == 0:
            return fast_body(spectrum, *rest)
        return body(spectrum, *rest)

    return jax.shard_map(
        pick,
        mesh=mesh,
        in_specs=(P(None, "depth", "plane", None), P(), P()),
        out_specs=(P("depth", "plane", None), P(None, None, "plane", "depth")),
        check_vma=False,
    )
```
